256 devices in a mesh: dp: 16 (over y, z_lo), mp: 4 (over x), expert: 4 (over z_hi, core).
Axes of the slice: x: 4, y: 4, z: 8 (z_hi: 2, z_lo: 4; z = z_hi * 4 + z_lo), core: 2. Of those that a mesh axis runs over, the one named last changes fastest.
Arguments:
- tokens: bfloat16 [24576, 1536], P(('dp', 'expert')), may hold values from -24 to 24
- segments: int32 [24576], replicated, may hold values from 0 to 47, never falling along the last dimension, each value on 1 to 1024 neighbouring positions
- norm_gains: float32 [2, 1536], replicated, may hold values from 0.1 to 1.9
- query_weight: bfloat16 [1536, 1536], P(None, 'mp'), may hold values from -8 to 8
- key_value_matrix: bfloat16 [2, 1536, 256], replicated, may hold values from -1 to 1
- output_weight: bfloat16 [1536, 1536], P('mp'), may hold values from -1 to 1
- trainer_gateup: float32 [16, 1536, 1536], P(('mp', 'expert'), 'dp'), may hold values from -0.15625 to 0.15625
- trainer_down: float32 [16, 768, 1536], P(('mp', 'expert'), 'dp'), may hold values from -0.21875 to 0.21875
- routes: int32 [24576, 4], P(('dp', 'expert')), may hold values from 0 to 15, all different within a row; in each aligned block of 96 rows (0 to 95, 96 to 191, ...) at most 48 rows name the same one
- route_weights: float32 [24576, 4], P(('dp', 'expert')), may hold values from 0.05 to 0.6
Outputs:
- layer_out: bfloat16 [64, 4, 96, 1536], P(('dp', 'expert'), 'mp')
The draws below stay inside these ranges and needn't reach their ends.
Inputs may be any that keep to these rules, and one draw needn't show every extreme that they name: `segments`: prompt numbers never fall along the positions; each prompt covers 1 to 1024 positions, and one covers exactly 1024. `routes`: the 4 experts of a token differ; in each aligned block of 96 rows no expert is named more than 48 times, a bound that some block reaches.
All inputs are finite; a program needn't handle non-finite values.
Results may differ from the reference program's by a relative error of at most 0.014.
Values may be sent and summed in bfloat16 or wider, within the bound.
A program may use at most 64 MiB of HBM per device.

```python
import math
import jax
import jax.numpy as jnp
import numpy as np
from jax import lax

MODEL_WIDTH = 1536
QUERY_HEADS = 12
KEY_VALUE_HEADS = 2
HEAD_SIZE = 128
FF = 768
TOPK = 4
PROMPT_MAX = 1024
PIECE_TOKENS = 384
EXPERTS = 16
TOKENS = 24576
PROMPTS = 48
BACK = 3
CAP = 48
N_DP = 16
N_MP = 4
N_EXPERT = 4


def shared_pairs(key):
    sampled_values = jax.random.normal(jax.random.fold_in(key, 11), (KEY_VALUE_HEADS, MODEL_WIDTH, 2 * HEAD_SIZE), jnp.float32) * MODEL_WIDTH ** (-0.5)
    return jnp.clip(sampled_values, -1.0, 1.0)


def draw_tokens(key, part):
    sampled_values = jax.random.normal(jax.random.fold_in(key, 5), (TOKENS, MODEL_WIDTH), jnp.float32)
    return jnp.clip(sampled_values, -24.0, 24.0).astype(jnp.bfloat16)


def draw_key_value_matrix(key, part):
    return shared_pairs(key).astype(jnp.bfloat16)


def draw_query_weight(key, part):
    jitter = jax.random.normal(jax.random.fold_in(key, 13), (MODEL_WIDTH, QUERY_HEADS * HEAD_SIZE), jnp.float32) * MODEL_WIDTH ** (-0.5)
    return jnp.clip(jitter, -8.0, 8.0).astype(jnp.bfloat16)


def level_of(stream_key, extent, shards, least, high):
    def one(dim, parts):
        steps = jax.random.uniform(jax.random.fold_in(jax.random.fold_in(stream_key, 6), dim), (parts,), jnp.float32, least / len(shards), high / len(shards))
        return jnp.repeat(jnp.exp(steps), extent[dim] // parts).reshape((-1,) + (1,) * (len(extent) - dim - 1))

    factor_of = one(*shards[0])
    for cut in shards[1:]:
        factor_of = factor_of * one(*cut)
    return factor_of


def split_up(amount, total, most, slope):
    weights = [(1 << 20) // math.isqrt(grade ** slope) + 1 for grade in range(2, amount + 1)]
    surplus, holding = total - most - (amount - 1), [1] * (amount - 1)
    while surplus > 0:
        candidates = [i for i in range(amount - 1) if holding[i] < most]
        mass, budget = sum([weights[i] for i in candidates]), surplus
        for i in candidates:
            addition = min(most - holding[i], max(1, budget * weights[i] // mass), surplus)
            holding[i] = holding[i] + addition
            surplus = surplus - addition
    return np.array([most] + holding)


def ragged(key, amount, total, bound, slope):
    if amount == 2:
        one = jax.random.randint(key, (), max(1, total - bound), min(bound, total - 1) + 1)
        return jnp.stack([one, total - one])
    lengths = jnp.asarray(split_up(amount, total, bound, slope), jnp.int32)
    twos = (amount - 1) // 2
    source_of, receiver = lengths[1:1 + 2 * twos:2], lengths[2:2 + 2 * twos:2]
    slack = jnp.minimum(source_of - 1, bound - receiver)
    passed = jax.random.randint(jax.random.fold_in(key, 1), (twos,), 0, 1 << 20) % (slack + 1)
    lengths = lengths.at[1:1 + 2 * twos:2].set(source_of - passed).at[2:2 + 2 * twos:2].set(receiver + passed)
    return lengths[jax.random.permutation(jax.random.fold_in(key, 2), amount)]


def assign_block(rng, own, number, rows, count, top, limit, slope):
    ranking = jax.random.permutation(rng, count)
    crowded, common = load_shares(count, rows * top, limit, slope, True), load_shares(count, rows * top, limit, slope, False)
    places = jnp.arange(count)

    def named(tallies, offset_by):
        used = int((tallies > 0).sum())
        fixed = max(1, used // 4)
        shifted = fixed + (places - fixed + offset_by * (used - fixed)) % max(1, count - fixed)
        return jnp.zeros((count,), jnp.int32).at[ranking[jnp.where(places < fixed, places, shifted)]].set(jnp.asarray(tallies, jnp.int32))

    tallies = jnp.where(number % 4 == 0, named(crowded, number // 4), named(common, number - number // 4 - 1))
    mixed = jax.random.permutation(jax.random.fold_in(own, 3), count)
    giver, sink = mixed[0:count // 2 * 2:2], mixed[1:count // 2 * 2:2]
    margin = jnp.minimum(tallies[giver] - 1, limit - tallies[sink]) // 2
    margin = jnp.where((giver == ranking[0]) | (sink == ranking[0]) | (tallies[sink] == 0), 0, jnp.maximum(margin, 0))
    shifted = jax.random.randint(jax.random.fold_in(own, 4), (count // 2,), 0, 1 << 20) % (margin + 1)
    tallies = tallies.at[giver].add(-shifted).at[sink].add(shifted)
    items = jnp.searchsorted(jnp.cumsum(tallies), jnp.arange(rows * top), side="right").astype(jnp.int32)
    grid = items.reshape(top, rows).T
    grid = grid[jax.random.permutation(jax.random.fold_in(own, 1), rows)]
    offset_by = jax.random.randint(jax.random.fold_in(own, 2), (rows, 1), 0, top)
    return jnp.take_along_axis(grid, (jnp.arange(top)[None, :] + offset_by) % top, axis=1)


def load_shares(number_of, total, most, slope, full):
    weights = [(1 << 20) // math.isqrt(grade ** slope) + 1 for grade in range(1, number_of + 1)]
    largest = most if full else min(most, max(-(-total // number_of), total * weights[0] // sum(weights)))
    least = 1 if total - largest >= number_of - 1 else 0
    holding, rest = [largest] + [least] * (number_of - 1), total - largest - least * (number_of - 1)
    while rest > 0:
        candidates = [i for i in range(1, number_of) if holding[i] < largest] or [i for i in range(1, number_of) if holding[i] < most]
        whole, remaining = sum([weights[i] for i in candidates]), rest
        for i in candidates:
            extra = min(most - holding[i], max(1, remaining * weights[i] // whole), rest)
            holding[i] = holding[i] + extra
            rest = rest - extra
    return np.array(holding)


def noise(rng, extent, scale, limit, split=(), kind=jnp.bfloat16):
    factor_of = level_of(rng, extent, split, -0.22, 0.18) if split else 1.0
    values = jax.random.normal(rng, extent, jnp.float32) * scale * factor_of
    return jnp.minimum(jnp.maximum(values, -limit), limit).astype(kind)


def setup_inputs(seed: int = 0) -> dict:
    streams_of = jax.random.split(jax.random.key(seed), 11)
    tokens = draw_tokens(jax.random.fold_in(streams_of[10], 71), 0)
    segments = jnp.searchsorted(jnp.cumsum(ragged(streams_of[1], PROMPTS, TOKENS, PROMPT_MAX, 1)), jnp.arange(TOKENS), side="right").astype(jnp.int32)
    norm_gains = jnp.clip(1.0 + 0.18 * jax.random.normal(streams_of[2], (2, MODEL_WIDTH), jnp.float32), 0.1, 1.9)
    query_weight = draw_query_weight(jax.random.fold_in(streams_of[10], 71), 0)
    key_value_matrix = draw_key_value_matrix(jax.random.fold_in(streams_of[10], 71), 0)
    output_weight = noise(streams_of[5], (QUERY_HEADS * HEAD_SIZE, MODEL_WIDTH), (HEAD_SIZE // 4) ** -0.5, 1.0, ((0, 4),))
    trainer_gateup = noise(streams_of[6], (EXPERTS, MODEL_WIDTH, 2 * FF), MODEL_WIDTH ** -0.5, 0.15625, ((0, 16), (1, 16)), jnp.float32)
    trainer_down = noise(streams_of[7], (EXPERTS, FF, MODEL_WIDTH), FF ** -0.5, 0.21875, ((0, 16), (1, 16)), jnp.float32)
    routes_keys = jax.random.split(jax.random.fold_in(streams_of[8], 1), TOKENS // (PIECE_TOKENS // N_MP))
    routes_turns = jax.random.permutation(jax.random.fold_in(streams_of[8], 3), TOKENS // (PIECE_TOKENS // N_MP))
    routes = jax.vmap(lambda own, number: assign_block(jax.random.fold_in(streams_of[8], 2), own, number, PIECE_TOKENS // N_MP, EXPERTS, TOPK, CAP, 2))(routes_keys, routes_turns).reshape((TOKENS, TOPK))
    route_weights = jnp.clip(0.05 + 0.55 * jax.random.uniform(streams_of[9], (TOKENS, TOPK), jnp.float32) ** level_of(streams_of[9], (TOKENS, TOPK), ((0, 64),), -0.2, 0.2), 0.05, 0.6)
    return dict(tokens=tokens, segments=segments, norm_gains=norm_gains, query_weight=query_weight, key_value_matrix=key_value_matrix, output_weight=output_weight, trainer_gateup=trainer_gateup, trainer_down=trainer_down, routes=routes, route_weights=route_weights)


def rms_scale(values, scaling):
    widened = values.astype(jnp.float32)
    return widened * lax.rsqrt(lax.optimization_barrier(jnp.mean(widened * widened, axis=-1, keepdims=True)) + 1e-06) * scaling

def slot_index(chosen, experts_count, capacity):
    flattened = chosen.reshape(-1)
    onehot = (flattened[:, None] == jnp.arange(experts_count, dtype=jnp.int32)[None, :]).astype(jnp.int32)
    before = jnp.cumsum(onehot, axis=0) - onehot
    return flattened * capacity + lax.optimization_barrier(jnp.sum(before * onehot, axis=1))

def reference(tokens, segments, norm_gains, query_weight, key_value_matrix, output_weight, trainer_gateup, trainer_down, routes, route_weights):
    server_gateup = trainer_gateup.astype(jnp.bfloat16)
    server_down = trainer_down.astype(jnp.bfloat16)
    normalized_input = rms_scale(tokens, norm_gains[0]).astype(jnp.bfloat16)
    query_rows = jnp.dot(normalized_input, query_weight, preferred_element_type=jnp.float32).astype(jnp.bfloat16)
    key_value_rows = jnp.stack([jnp.dot(normalized_input, key_value_matrix[head_group_index], preferred_element_type=jnp.float32).astype(jnp.bfloat16) for head_group_index in range(KEY_VALUE_HEADS)])
    common_pairs = QUERY_HEADS // KEY_VALUE_HEADS
    window = (BACK + 1) * PIECE_TOKENS

    def attend(block_index):
        query_offset = block_index * PIECE_TOKENS
        key_start = jnp.maximum(query_offset - BACK * PIECE_TOKENS, 0)
        query_block_rows = lax.dynamic_slice_in_dim(query_rows, query_offset, PIECE_TOKENS, 0).astype(jnp.float32).reshape(PIECE_TOKENS, KEY_VALUE_HEADS, common_pairs, HEAD_SIZE)
        block_pairs = lax.dynamic_slice_in_dim(key_value_rows, key_start, window, 1).astype(jnp.float32)
        query_pos = query_offset + jnp.arange(PIECE_TOKENS, dtype=jnp.int32)
        key_pos = key_start + jnp.arange(window, dtype=jnp.int32)
        query_segment = lax.dynamic_slice_in_dim(segments, query_offset, PIECE_TOKENS, 0)
        key_segment = lax.dynamic_slice_in_dim(segments, key_start, window, 0)
        allowed = (query_segment[:, None] == key_segment[None, :]) & (key_pos[None, :] <= query_pos[:, None])
        scores = jnp.einsum('rgsd,gnd->gsrn', query_block_rows, block_pairs[:, :, :HEAD_SIZE]) / math.sqrt(HEAD_SIZE)
        highest = lax.optimization_barrier(jnp.max(jnp.where(allowed, scores, -1e+30), axis=-1, keepdims=True))
        weights = jnp.where(allowed, jnp.exp(scores - highest), 0.0)
        denominator = lax.optimization_barrier(jnp.sum(weights, axis=-1))
        rounded = lax.optimization_barrier(weights.astype(jnp.bfloat16)).astype(jnp.float32)
        mixture = jnp.einsum('gsrn,gnd->gsrd', rounded, block_pairs[:, :, HEAD_SIZE:]) / denominator[..., None]
        return jnp.transpose(mixture, (2, 0, 1, 3)).reshape(PIECE_TOKENS, QUERY_HEADS * HEAD_SIZE).astype(jnp.bfloat16)
    attended = lax.map(attend, jnp.arange(TOKENS // PIECE_TOKENS, dtype=jnp.int32)).reshape(TOKENS, QUERY_HEADS * HEAD_SIZE)
    attention_out = jnp.dot(attended, output_weight, preferred_element_type=jnp.float32)
    middle = (tokens.astype(jnp.float32) + attention_out).astype(jnp.bfloat16)
    expert_input = rms_scale(middle, norm_gains[1]).astype(jnp.bfloat16)
    part_rows = PIECE_TOKENS // N_MP
    gateup_wide = server_gateup.astype(jnp.float32)
    down_wide = server_down.astype(jnp.float32)

    def experts_block(operands):
        block_rows, chosen, gate_values = operands
        slot_rows = slot_index(chosen, EXPERTS, CAP)
        buffer = jnp.zeros((EXPERTS * CAP, MODEL_WIDTH), jnp.bfloat16).at[slot_rows].set(jnp.repeat(block_rows, TOPK, axis=0)).reshape(EXPERTS, CAP, MODEL_WIDTH)
        projected = jnp.einsum('ecd,edf->ecf', buffer.astype(jnp.float32), gateup_wide)
        hidden = (jax.nn.relu(projected[..., :FF]) * projected[..., FF:]).astype(jnp.bfloat16)
        expert_out = jnp.einsum('ecf,efd->ecd', hidden.astype(jnp.float32), down_wide).astype(jnp.bfloat16)
        picked = expert_out.reshape(EXPERTS * CAP, MODEL_WIDTH)[slot_rows].reshape(part_rows, TOPK, MODEL_WIDTH).astype(jnp.float32)
        return lax.optimization_barrier(jnp.sum(gate_values[..., None] * picked, axis=1))
    expert_sum = lax.map(experts_block, (expert_input.reshape(-1, part_rows, MODEL_WIDTH), routes.reshape(-1, part_rows, TOPK), route_weights.reshape(-1, part_rows, TOPK)))
    layer = (middle.astype(jnp.float32) + expert_sum.reshape(TOKENS, MODEL_WIDTH)).astype(jnp.bfloat16)
    return layer.reshape(N_DP * N_EXPERT, N_MP, part_rows, MODEL_WIDTH)
```

```python
import functools
import heapq
import math

import jax
import jax.numpy as jnp
from jax import lax
from jax.experimental import pallas as pl
from jax.experimental.pallas import tpu as pltpu
from jax.sharding import PartitionSpec as P

MODEL_WIDTH = 1536
QUERY_HEADS = 12
KEY_VALUE_HEADS = 2
HEAD_SIZE = 128
FF = 768
TOPK = 4
PROMPT_MAX = 1024


LINKS = ("y+", "y-", "z+", "z-")
AXES = ("dp", "mp", "expert")
MESH = pl.DeviceIdType.MESH


def column_ring(moves, rank, tag, piece, halves, dy, have):
    got = {0: have}
    up, down = have, have
    for s in range(1, 4):
        moves.append(("z+", (dy, 1 - s), piece, up, (rank, tag, s)))
        up = got[-s] = [len(moves) - 1]
        moves.append(("z-", (dy, s - 1), piece, down, (rank, tag, s)))
        down = got[s] = [len(moves) - 1]
    moves.append(("z+", (dy, -3), halves[0], up, (rank, tag, 4)))
    moves.append(("z-", (dy, 3), halves[1], down, (rank, tag, 4)))
    got[4] = [len(moves) - 2, len(moves) - 1]
    return got


def row_ring(moves, rank, tag, piece, halves, dz, have, late):
    start = len(moves)
    moves.append(("y+", (0, dz), piece, have, (rank, tag, 1 + late)))
    moves.append(("y-", (0, dz), piece, have, (rank, tag, 1 + late)))
    moves.append(("y+", (-1, dz), halves[0], [start], (rank, tag, 2 + late)))
    moves.append(("y-", (1, dz), halves[1], [start + 1], (rank, tag, 2 + late)))
    return {0: have, -1: [start], 1: [start + 1], 2: [start + 2, start + 3]}


def gather_moves(pieces):
    moves = []
    for rank, order, piece, halves in pieces:
        if order == "zy":
            got = column_ring(moves, rank, 0, piece, halves, 0, [])
            for late, dz in enumerate((0, -1, 1, -2, 2, -3, 3, 4)):
                row_ring(moves, rank, 1, piece, halves, dz, got[dz], late)
        else:
            got = row_ring(moves, rank, 0, piece, halves, 0, [], 0)
            for late, dy in enumerate((0, -1, 1, 2)):
                column_ring(moves, rank, 1 + late, piece, halves, dy, got[dy])
    return moves


def gather_program(moves, depth, rate=46.5e3, latency=1.7):
    issued, got = set(), set()
    free, flying = dict.fromkeys(LINKS, 0.0), dict.fromkeys(LINKS, 0)
    arrivals, now, program = [], 0.0, []
    while True:
        for link in LINKS:
            while flying[link] < depth:
                ready = [
                    (moves[i][4], i)
                    for i in range(len(moves))
                    if moves[i][0] == link and i not in issued and got.issuperset(moves[i][3])
                ]
                if not ready:
                    break
                i = min(ready)[1]
                _, r0, r1, c0, c1 = moves[i][2]
                issued.add(i)
                flying[link] += 1
                program.append(("send", i, now))
                free[link] = max(now, free[link]) + (r1 - r0) * (c1 - c0) * 2 / rate
                heapq.heappush(arrivals, (free[link] + latency, i))
        if not arrivals:
            return program
        now, i = heapq.heappop(arrivals)
        got.add(i)
        flying[moves[i][0]] -= 1
        program.append(("recv", i, now))


PIECES = (
    (0, "zy", ("gu", 0, 96, 0, 1536), (("gu", 0, 48, 0, 1536), ("gu", 48, 96, 0, 1536))),
    (0, "yz", ("dn", 0, 48, 0, 1536), (("dn", 0, 48, 0, 768), ("dn", 0, 48, 768, 1536))),
)


def gather_kernel(moves, program, gu_own, dn_own, gu_all, dn_all, own_sem, send_sem, recv_sem):
    dp, mp, expert = (lax.axis_index(a) for a in AXES)
    y, z_lo, z_hi, core = dp // 4, dp % 4, expert // 2, expert % 2
    z = z_hi * 4 + z_lo

    def place(dy, dz):
        other_y, other_z = (y + dy + 8) % 4, (z + dz + 8) % 8
        return other_z // 4, other_y * 4 + other_z % 4

    def device(dy, dz):
        half, index = place(dy, dz)
        return (index, mp, half * 2 + core)

    target = {"y+": (1, 0), "y-": (-1, 0), "z+": (0, 1), "z-": (0, -1)}
    own, whole = {"gu": gu_own, "dn": dn_own}, {"gu": gu_all, "dn": dn_all}

    barrier = pltpu.get_barrier_semaphore()
    for link in LINKS:
        pl.semaphore_signal(barrier, inc=1, device_id=device(*target[link]), device_id_type=MESH)
    pl.semaphore_wait(barrier, 4)

    def copy(i):
        link, (dy, dz), (name, r0, r1, c0, c1), _, _ = moves[i]
        half, index = place(dy, dz)
        rows, columns = pl.ds(r0, r1 - r0), pl.ds(c0, c1 - c0)
        landing = whole[name].at[half, index, rows, columns]
        start = own[name].at[rows, columns] if (dy, dz) == (0, 0) else landing
        return pltpu.make_async_remote_copy(
            src_ref=start,
            dst_ref=landing,
            send_sem=send_sem.at[i],
            recv_sem=recv_sem.at[i],
            device_id=device(*target[link]),
            device_id_type=MESH,
        )

    half, index = place(0, 0)
    kept = [
        pltpu.make_async_copy(own[name], whole[name].at[half, index], own_sem.at[k])
        for k, name in enumerate(("gu", "dn"))
    ]
    for c in kept:
        c.start()
    for kind, i, _ in program:
        if kind == "send":
            copy(i).start()
        else:
            copy(i).wait_recv()
    for i in range(len(moves)):
        copy(i).wait_send()
    for c in kept:
        c.wait()


def gather_weights(gateup, down):
    moves = gather_moves(PIECES)
    program = gather_program(moves, 4)
    return pl.pallas_call(
        functools.partial(gather_kernel, moves, program),
        out_shape=[
            jax.ShapeDtypeStruct((2, 16) + gateup.shape, jnp.bfloat16),
            jax.ShapeDtypeStruct((2, 16) + down.shape, jnp.bfloat16),
        ],
        in_specs=[pl.BlockSpec(memory_space=pl.ANY)] * 2,
        out_specs=[pl.BlockSpec(memory_space=pl.ANY)] * 2,
        scratch_shapes=[
            pltpu.SemaphoreType.DMA((2,)),
            pltpu.SemaphoreType.DMA((len(moves),)),
            pltpu.SemaphoreType.DMA((len(moves),)),
        ],
        compiler_params=pltpu.CompilerParams(collective_id=0, has_side_effects=True),
    )(gateup, down)


def shifted(value, axis, steps):
    count = lax.axis_size(axis)
    initial, last = (max(0, -steps), min(count, count - steps))
    return lax.ppermute(value, axis, [(source, source + steps) for source in range(initial, last)])


def rms_scale(values, scaling):
    widened = values.astype(jnp.float32)
    return (
        widened * lax.rsqrt(jnp.mean(widened * widened, axis=-1, keepdims=True) + 1e-06) * scaling
    )


def slot_index(chosen, experts_count, capacity):
    flattened = chosen.reshape(-1)
    onehot = (flattened[:, None] == jnp.arange(experts_count, dtype=jnp.int32)[None, :]).astype(
        jnp.int32
    )
    before = jnp.cumsum(onehot, axis=0) - onehot
    return flattened * capacity + jnp.sum(before * onehot, axis=1)


def body(
    tokens,
    segments,
    norm_gains,
    query_weight,
    key_value_matrix,
    output_weight,
    trainer_gateup,
    trainer_down,
    routes,
    route_weights,
):
    both_gateup, both_down = gather_weights(
        trainer_gateup[0].astype(jnp.bfloat16), trainer_down[0].astype(jnp.bfloat16)
    )
    half = lax.axis_index("expert") // 2
    gateup_full, down_full = (
        lax.dynamic_index_in_dim(both, half, 0, keepdims=True).reshape(1, -1, MODEL_WIDTH)
        for both in (both_gateup, both_down)
    )
    own_rows = tokens.shape[0]
    head_group_index = lax.axis_index(("dp", "expert"))
    column_position = lax.axis_index("mp")
    first_row = head_group_index * own_rows
    local_heads = query_weight.shape[1] // HEAD_SIZE
    normalized_input = rms_scale(tokens, norm_gains[0]).astype(jnp.bfloat16)
    query_rows = jnp.dot(normalized_input, query_weight, preferred_element_type=jnp.float32).astype(
        jnp.bfloat16
    )
    paired_head_index = column_position * local_heads // (QUERY_HEADS // KEY_VALUE_HEADS)
    pair_weight = lax.dynamic_index_in_dim(key_value_matrix, paired_head_index, 0, keepdims=False)
    key_values = jnp.dot(normalized_input, pair_weight, preferred_element_type=jnp.float32).astype(
        jnp.bfloat16
    )
    query_pos = first_row + jnp.arange(own_rows, dtype=jnp.int32)
    query_segment = lax.dynamic_slice_in_dim(segments, first_row, own_rows, 0)
    shaped_queries = query_rows.reshape(own_rows, local_heads, HEAD_SIZE)
    start_state = (
        jnp.full((local_heads, own_rows), -1e30, jnp.float32),
        jnp.zeros((local_heads, own_rows), jnp.float32),
        jnp.zeros((local_heads, own_rows, HEAD_SIZE), jnp.float32),
    )
    pieces_back = (PROMPT_MAX - 1) // own_rows + 1
    earlier = [key_values]
    for offset in range(1, pieces_back + 1):
        earlier.insert(0, shifted(key_values, ("dp", "expert"), offset))
    key_pos = (
        first_row
        - pieces_back * own_rows
        + jnp.arange((pieces_back + 1) * own_rows, dtype=jnp.int32)
    )
    key_segment = jnp.where(key_pos >= 0, segments[jnp.maximum(key_pos, 0)], -1)
    block_pairs = jnp.concatenate(earlier, axis=0)
    highest, denominator, accumulated = start_state
    scores = jnp.einsum(
        "rhd,nd->hrn",
        shaped_queries,
        block_pairs[:, :HEAD_SIZE],
        preferred_element_type=jnp.float32,
    ) / math.sqrt(HEAD_SIZE)
    allowed = (
        (query_segment[:, None] == key_segment[None, :]) & (key_pos[None, :] <= query_pos[:, None])
    )[None]
    newest = jnp.maximum(highest, jnp.max(jnp.where(allowed, scores, -1e30), axis=-1))
    weights = jnp.where(allowed, jnp.exp(scores - newest[..., None]), 0.0)
    denominator = jnp.sum(weights, axis=-1)
    accumulated = jnp.einsum(
        "hrn,nd->hrd",
        weights.astype(jnp.bfloat16),
        block_pairs[:, HEAD_SIZE:],
        preferred_element_type=jnp.float32,
    )
    carried = (newest, denominator, accumulated)
    highest, denominator, accumulated = carried
    attended = (
        jnp.transpose(accumulated / denominator[..., None], (1, 0, 2))
        .reshape(own_rows, local_heads * HEAD_SIZE)
        .astype(jnp.bfloat16)
    )
    part_rows = own_rows // lax.axis_size("mp")
    attention_out = lax.psum_scatter(
        jnp.dot(attended, output_weight, preferred_element_type=jnp.float32).astype(jnp.bfloat16),
        "mp",
        scatter_dimension=0,
        tiled=True,
    ).astype(jnp.float32)
    part_start = column_position * part_rows
    middle = (
        lax.dynamic_slice_in_dim(tokens, part_start, part_rows, 0).astype(jnp.float32)
        + attention_out
    ).astype(jnp.bfloat16)
    expert_input = rms_scale(middle, norm_gains[1]).astype(jnp.bfloat16)
    chosen = lax.dynamic_slice_in_dim(routes, part_start, part_rows, 0)
    gate_values = lax.dynamic_slice_in_dim(route_weights, part_start, part_rows, 0)
    experts_count = lax.axis_size(("mp", "expert"))
    capacity = 2 * part_rows * TOPK // experts_count
    slot_rows = slot_index(chosen, experts_count, capacity)
    buffer = (
        jnp.zeros((experts_count * capacity, MODEL_WIDTH), jnp.bfloat16)
        .at[slot_rows]
        .set(jnp.repeat(expert_input, TOPK, axis=0))
        .reshape(experts_count, capacity, MODEL_WIDTH)
    )
    received = lax.all_to_all(buffer, ("mp", "expert"), split_axis=0, concat_axis=0, tiled=True)
    senders = received.shape[0]
    slots_here = received.shape[1]
    projected = jnp.dot(
        received.reshape(senders * slots_here, MODEL_WIDTH),
        gateup_full[0],
        preferred_element_type=jnp.float32,
    )
    hidden = (jax.nn.relu(projected[:, :FF]) * projected[:, FF:]).astype(jnp.bfloat16)
    produced = (
        jnp.dot(hidden, down_full[0], preferred_element_type=jnp.float32)
        .astype(jnp.bfloat16)
        .reshape(senders, slots_here, MODEL_WIDTH)
    )
    returned = lax.all_to_all(produced, ("mp", "expert"), split_axis=0, concat_axis=0, tiled=True)
    picked = (
        returned.reshape(experts_count * capacity, MODEL_WIDTH)[slot_rows]
        .reshape(part_rows, TOPK, MODEL_WIDTH)
        .astype(jnp.float32)
    )
    layer = (middle.astype(jnp.float32) + jnp.sum(gate_values[..., None] * picked, axis=1)).astype(
        jnp.bfloat16
    )
    return layer.reshape(1, 1, part_rows, MODEL_WIDTH)


def solution(mesh):
    in_specs = (
        P(("dp", "expert"), None),
        P(),
        P(),
        P(None, "mp"),
        P(),
        P("mp", None),
        P(("mp", "expert"), "dp", None),
        P(("mp", "expert"), "dp", None),
        P(("dp", "expert"), None),
        P(("dp", "expert"), None),
    )
    out_specs = P(("dp", "expert"), "mp", None, None)
    return jax.shard_map(body, mesh=mesh, in_specs=in_specs, out_specs=out_specs, check_vma=False)
```

```python
import functools
import heapq
import math
import types

import jax
import jax.numpy as jnp
from jax import lax
from jax.experimental import pallas as pl
from jax.experimental.pallas import tpu as pltpu
from jax.sharding import PartitionSpec as P

MODEL_WIDTH = 1536
FF = 768
TOPK = 4


LINKS = ("y+", "y-", "z+", "z-")
AXES = ("dp", "mp", "expert")
MESH = pl.DeviceIdType.MESH


def column_ring(moves, rank, tag, piece, halves, dy, have):
    got = {0: have}
    up, down = have, have
    for s in range(1, 4):
        moves.append(("z+", (dy, 1 - s), piece, up, (rank, tag, s)))
        up = got[-s] = [len(moves) - 1]
        moves.append(("z-", (dy, s - 1), piece, down, (rank, tag, s)))
        down = got[s] = [len(moves) - 1]
    moves.append(("z+", (dy, -3), halves[0], up, (rank, tag, 4)))
    moves.append(("z-", (dy, 3), halves[1], down, (rank, tag, 4)))
    got[4] = [len(moves) - 2, len(moves) - 1]
    return got


def row_ring(moves, rank, tag, piece, halves, dz, have, late):
    start = len(moves)
    moves.append(("y+", (0, dz), piece, have, (rank, tag, 1 + late)))
    moves.append(("y-", (0, dz), piece, have, (rank, tag, 1 + late)))
    moves.append(("y+", (-1, dz), halves[0], [start], (rank, tag, 2 + late)))
    moves.append(("y-", (1, dz), halves[1], [start + 1], (rank, tag, 2 + late)))
    return {0: have, -1: [start], 1: [start + 1], 2: [start + 2, start + 3]}


def gather_moves(pieces):
    moves = []
    for rank, order, piece, halves in pieces:
        if order == "zy":
            got = column_ring(moves, rank, 0, piece, halves, 0, [])
            for late, dz in enumerate((0, -1, 1, -2, 2, -3, 3, 4)):
                row_ring(moves, rank, 1, piece, halves, dz, got[dz], late)
        else:
            got = row_ring(moves, rank, 0, piece, halves, 0, [], 0)
            for late, dy in enumerate((0, -1, 1, 2)):
                column_ring(moves, rank, 1 + late, piece, halves, dy, got[dy])
    return moves


def gather_program(moves, depth, rate=46.5e3, latency=1.7):
    issued, got = set(), set()
    free, flying = dict.fromkeys(LINKS, 0.0), dict.fromkeys(LINKS, 0)
    arrivals, now, program = [], 0.0, []
    while True:
        for link in LINKS:
            while flying[link] < depth:
                ready = [
                    (moves[i][4], i)
                    for i in range(len(moves))
                    if moves[i][0] == link and i not in issued and got.issuperset(moves[i][3])
                ]
                if not ready:
                    break
                i = min(ready)[1]
                _, r0, r1, c0, c1 = moves[i][2]
                issued.add(i)
                flying[link] += 1
                program.append(("send", i, now))
                free[link] = max(now, free[link]) + (r1 - r0) * (c1 - c0) * 2 / rate
                heapq.heappush(arrivals, (free[link] + latency, i))
        if not arrivals:
            return program
        now, i = heapq.heappop(arrivals)
        got.add(i)
        flying[moves[i][0]] -= 1
        program.append(("recv", i, now))


PIECES = (
    (0, "zy", ("gu", 0, 96, 0, 1024), (("gu", 0, 48, 0, 1024), ("gu", 48, 96, 0, 1024))),
    (0, "yz", ("gu", 0, 96, 1024, 1536), (("gu", 0, 48, 1024, 1536), ("gu", 48, 96, 1024, 1536))),
    (1, "zy", ("dn", 0, 48, 0, 768), (("dn", 0, 48, 0, 384), ("dn", 0, 48, 384, 768))),
    (1, "yz", ("dn", 0, 48, 768, 1536), (("dn", 0, 48, 768, 1152), ("dn", 0, 48, 1152, 1536))),
)
DEPTH = 6
PUMP = dict(
    start=0.1, kv=4, query=8, attend=(14, 16, 18), project=22, middle=34, dispatch=44,
    gather=(46, 47, 48, 49), gate=(54, 57, 60, 63, 66, 69),
)

ROWS = 384
PART = 96
SLOTS = 48
WINDOW = 1152
F_CHUNK = 256
N_CHUNK = 512
N_CHUNKS = MODEL_WIDTH // N_CHUNK


def dot(a, b):
    return jnp.dot(a, b, preferred_element_type=jnp.float32)


def layer_kernel(moves, program, refs):
    r = refs
    dp, mp, expert = (lax.axis_index(a) for a in AXES)
    y, z_lo, z_hi, core = dp // 4, dp % 4, expert // 2, expert % 2
    z = z_hi * 4 + z_lo
    group = dp * 4 + expert

    def place(dy, dz):
        other_y, other_z = (y + dy + 8) % 4, (z + dz + 8) % 8
        return other_z // 4, other_y * 4 + other_z % 4

    def grid_device(dy, dz):
        half, index = place(dy, dz)
        return (index, mp, half * 2 + core)

    def column_device(d):
        return (dp, (mp + d + 4) % 4, expert)

    def piece_device(d):
        other = (group + d + 64) % 64
        return (other // 4, mp, other % 4)

    partner = (dp, mp, z_hi * 2 + 1 - core)
    target = {"y+": (1, 0), "y-": (-1, 0), "z+": (0, 1), "z-": (0, -1)}

    barrier = pltpu.get_barrier_semaphore()
    greeted = [grid_device(*target[link]) for link in LINKS]
    greeted += [column_device(d) for d in (1, 2, 3)] + [piece_device(-d) for d in (1, 2, 3)]
    greeted.append(partner)
    for other in greeted:
        pl.semaphore_signal(barrier, inc=1, device_id=other, device_id_type=MESH)
    pl.semaphore_wait(barrier, len(greeted))

    def remote(start, landing, sems, i, device):
        return pltpu.make_async_remote_copy(
            src_ref=start,
            dst_ref=landing,
            send_sem=sems[0].at[i],
            recv_sem=sems[1].at[i],
            device_id=device,
            device_id_type=MESH,
        )

    own, whole = {"gu": r.gu_own, "dn": r.dn_own}, {"gu": r.gu, "dn": r.dn}

    def weight_copy(i):
        link, (dy, dz), (name, r0, r1, c0, c1), _, _ = moves[i]
        half, index = place(dy, dz)
        rows, columns = pl.ds(r0, r1 - r0), pl.ds(c0, c1 - c0)
        landing = whole[name].at[half, index, rows, columns]
        start = own[name].at[rows, columns] if (dy, dz) == (0, 0) else landing
        return remote(start, landing, r.weight_sems, i, grid_device(*target[link]))

    position = [0]

    def pump(until=None, needed=None):
        while position[0] < len(program):
            kind, i, when = program[position[0]]
            if until is not None and when > until:
                return
            if kind == "send":
                weight_copy(i).start()
            else:
                weight_copy(i).wait_recv()
                if needed is not None:
                    needed.discard(i)
            position[0] += 1
            if needed is not None and not needed:
                return

    half, index = place(0, 0)
    kept = [
        pltpu.make_async_copy(own[name], whole[name].at[half, index], r.own_sems.at[k])
        for k, name in enumerate(("gu", "dn"))
    ]
    for c in kept:
        c.start()
    routing = remote(r.routing, r.routing_other, r.routing_sems, 0, partner)
    routing.start()
    pump(PUMP["start"])

    gain = r.gains[0:1, :]

    @pl.loop(0, ROWS // 32)
    def _(i):
        rows = pl.ds(pl.multiple_of(i * 32, 32), 32)
        wide = r.tokens[rows, :].astype(jnp.float32)
        scale = lax.rsqrt(jnp.mean(wide * wide, axis=-1, keepdims=True) + 1e-6)
        r.normed[rows, :] = (wide * scale * gain).astype(jnp.bfloat16)

    r.pairs[WINDOW:, :] = dot(r.normed[...], r.pair_weight[mp // 2]).astype(jnp.bfloat16)

    def pair_copy(d):
        first = 128 if d == 3 else 0
        rows = ROWS - first
        return remote(
            r.pairs.at[pl.ds(WINDOW + first, rows), :],
            r.pairs.at[pl.ds(WINDOW - d * ROWS + first, rows), :],
            r.pair_sems,
            d - 1,
            piece_device(d),
        )

    for d in (1, 2, 3):
        pair_copy(d).start()
    pump(PUMP["kv"])
    r.queries[...] = dot(r.normed[...], r.query_weight[...]).astype(jnp.bfloat16)
    pump(PUMP["query"])

    lanes = []
    for k in range(12):
        row = (group * 3 - 9 + k + 192) % 192
        lanes.append(r.segments[pl.ds(row, 1), :])
    key_segment = jnp.concatenate(lanes, axis=1)
    diagonal = lax.broadcasted_iota(jnp.int32, (128, 128), 0) == lax.broadcasted_iota(
        jnp.int32, (128, 128), 1
    )
    first_key = (group - 3) * ROWS

    for d in (1, 2, 3):
        pair_copy(d).wait_recv()
    for c in range(3):
        low = (c + 1) * 128
        own_lanes = jnp.broadcast_to(lanes[9 + c].astype(jnp.float32), (128, 128))
        query_segment = jnp.sum(jnp.where(diagonal, own_lanes, 0.0), axis=1, keepdims=True)
        key_offset = low + lax.broadcasted_iota(jnp.int32, (128, WINDOW), 1)
        query_offset = WINDOW + c * 128 + lax.broadcasted_iota(jnp.int32, (128, WINDOW), 0)
        allowed = (
            (key_segment[:, low : low + WINDOW].astype(jnp.float32) == query_segment)
            & (key_offset <= query_offset)
            & (key_offset + first_key >= 0)
        )
        keys = r.pairs[low : low + WINDOW, :128]
        values = r.pairs[low : low + WINDOW, 128:]
        for h in range(3):
            query = r.queries[c * 128 : (c + 1) * 128, h * 128 : (h + 1) * 128]
            scores = lax.dot_general(
                query, keys, (((1,), (1,)), ((), ())), preferred_element_type=jnp.float32
            )
            scores = jnp.where(allowed, scores * (1.0 / math.sqrt(128)), -1e30)
            weights = jnp.exp(scores - jnp.max(scores, axis=1, keepdims=True))
            total = jnp.sum(weights, axis=1, keepdims=True)
            mixed = dot(weights.astype(jnp.bfloat16), values) / total
            r.attended[c * 128 : (c + 1) * 128, h * 128 : (h + 1) * 128] = mixed.astype(jnp.bfloat16)
        pump(PUMP["attend"][c])

    def partial_copy(d):
        return remote(
            r.projected.at[(mp + d) % 4], r.projected_in.at[d - 1], r.projected_sems, d - 1, column_device(d)
        )

    r.projected[...] = (
        dot(r.attended[...], r.output_weight[...]).astype(jnp.bfloat16).reshape(4, PART, MODEL_WIDTH)
    )
    pump(PUMP["project"])
    for d in (2, 1, 3):
        partial_copy(d).start()

    routing.wait_recv()
    earlier = (
        lax.broadcasted_iota(jnp.int32, (PART, PART), 0) < lax.broadcasted_iota(jnp.int32, (PART, PART), 1)
    ).astype(jnp.bfloat16)
    slot = lax.broadcasted_iota(jnp.int32, (SLOTS, PART), 0).astype(jnp.float32)
    served = [(mp * 4 + e * 2 + core).astype(jnp.float32) for e in range(2)]
    for d in range(4):
        m = (mp - d + 4) % 4
        for side, table in enumerate((r.routing, r.routing_other)):
            routes, gates = table[m, 0:4, :], table[m, 4:8, :]
            for e in range(2):
                named = routes == served[e]
                hit = jnp.sum(jnp.where(named, 1.0, 0.0), axis=0, keepdims=True)
                gate = jnp.sum(jnp.where(named, gates, 0.0), axis=0, keepdims=True)
                rank = dot(jnp.broadcast_to(hit, (8, PART)).astype(jnp.bfloat16), earlier)[0:1, :]
                chosen = jnp.where((slot == rank) & (hit > 0.5), 1.0, 0.0)
                r.slots[d, side, e * SLOTS : (e + 1) * SLOTS, :] = chosen.astype(jnp.bfloat16)
                r.slot_gates[e, d, side * SLOTS : (side + 1) * SLOTS, :] = jnp.sum(
                    chosen * gate, axis=1, keepdims=True
                )
    pump(PUMP["middle"])

    for d in (1, 2, 3):
        partial_copy(d).wait_recv()
    summed = r.tokens[pl.ds(pl.multiple_of(mp * PART, PART), PART), :].astype(jnp.float32)
    attention = r.projected[mp].astype(jnp.float32)
    for d in range(3):
        attention = attention + r.projected_in[d].astype(jnp.float32)
    middle = (summed + attention).astype(jnp.bfloat16)
    r.middle[...] = middle
    wide = middle.astype(jnp.float32)
    scale = lax.rsqrt(jnp.mean(wide * wide, axis=-1, keepdims=True) + 1e-6)
    r.states[0, 0] = (wide * scale * r.gains[1:2, :]).astype(jnp.bfloat16)

    def state_copy(d):
        return remote(r.states.at[0, 0], r.states.at[0, d], r.state_sems, d - 1, column_device(d))

    def across_copy(d):
        return remote(r.states.at[0, d], r.states.at[1, d], r.across_sems, d, partner)

    for d in (2, 1, 3):
        state_copy(d).start()
    across_copy(0).start()
    pump(PUMP["dispatch"])
    for step, d in enumerate((0, 1, 3, 2)):
        if d:
            state_copy(d).wait_recv()
            across_copy(d).start()
        for side in range(2):
            if side:
                across_copy(d).wait_recv()
            picked = dot(r.slots[d, side], r.states[side, d]).astype(jnp.bfloat16)
            for e in range(2):
                r.routed[e, d, side * SLOTS : (side + 1) * SLOTS, :] = picked[e * SLOTS : (e + 1) * SLOTS]
        pump(PUMP["gather"][step])

    for k in range(2):
        kept[k].wait()
    arrived = {i for kind, i, _ in program[: position[0]] if kind == "recv"}
    missing = {i for i, move in enumerate(moves) if move[2][0] == "gu"} - arrived
    if missing:
        pump(needed=missing)
    for e in range(2):
        inputs = r.routed[e].reshape(4 * PART, MODEL_WIDTH)
        for f in range(3):
            left = f * F_CHUNK
            gate = dot(inputs, r.gu[e, :, :, left : left + F_CHUNK].reshape(MODEL_WIDTH, F_CHUNK))
            rise = dot(inputs, r.gu[e, :, :, FF + left : FF + left + F_CHUNK].reshape(MODEL_WIDTH, F_CHUNK))
            r.hidden[e, :, left : left + F_CHUNK] = (jnp.maximum(gate, 0.0) * rise).astype(jnp.bfloat16)
            pump(PUMP["gate"][e * 3 + f])
    pump()

    def return_core(n):
        columns = pl.ds(n * N_CHUNK, N_CHUNK)
        return remote(
            r.outgoing.at[1, :, :, columns], r.core_in.at[:, :, columns], r.core_sems, n, partner
        )

    def return_column(n, d):
        columns = pl.ds(n * N_CHUNK, N_CHUNK)
        return remote(
            r.merged.at[d, :, columns],
            r.column_in.at[d - 1, :, columns],
            r.column_sems,
            n * 3 + d - 1,
            column_device(-d),
        )

    def merge(n):
        columns = slice(n * N_CHUNK, (n + 1) * N_CHUNK)
        return_core(n).wait_recv()
        for d in (2, 1, 3, 0):
            both = r.outgoing[0, d, :, columns].astype(jnp.float32) + r.core_in[d, :, columns].astype(
                jnp.float32
            )
            r.merged[d, :, columns] = both.astype(jnp.bfloat16)
        for d in (2, 1, 3):
            return_column(n, d).start()

    for n in range(N_CHUNKS):
        columns = slice(n * N_CHUNK, (n + 1) * N_CHUNK)
        for e in range(2):
            produced = dot(r.hidden[e], r.dn[e, :, :, columns].reshape(FF, N_CHUNK))
            gates = r.slot_gates[e].reshape(4 * PART, 1)
            r.produced[e, :, :, :] = (produced * gates).astype(jnp.bfloat16).reshape(4, PART, N_CHUNK)
        for side in (1, 0):
            for d in range(4):
                rows = slice(side * SLOTS, (side + 1) * SLOTS)
                stacked = jnp.concatenate([r.produced[0, d, rows, :], r.produced[1, d, rows, :]], axis=0)
                back = lax.dot_general(
                    r.slots[d, side], stacked, (((0,), (0,)), ((), ())), preferred_element_type=jnp.float32
                )
                r.outgoing[side, d, :, columns] = back.astype(jnp.bfloat16)
            if side:
                return_core(n).start()
        if n:
            merge(n - 1)
    merge(N_CHUNKS - 1)
    for n in range(N_CHUNKS):
        columns = slice(n * N_CHUNK, (n + 1) * N_CHUNK)
        for d in (1, 2, 3):
            return_column(n, d).wait_recv()
        result = r.middle[:, columns].astype(jnp.float32) + r.merged[0, :, columns].astype(jnp.float32)
        for d in range(3):
            result = result + r.column_in[d, :, columns].astype(jnp.float32)
        r.out[:, columns] = result.astype(jnp.bfloat16)

    for i in range(len(moves)):
        weight_copy(i).wait_send()
    routing.wait_send()
    for d in (1, 2, 3):
        pair_copy(d).wait_send()
        partial_copy(d).wait_send()
        state_copy(d).wait_send()
    for d in range(4):
        across_copy(d).wait_send()
    for n in range(N_CHUNKS):
        return_core(n).wait_send()
        for d in (1, 2, 3):
            return_column(n, d).wait_send()


INPUTS = ("tokens", "segments", "gains", "query_weight", "pair_weight", "output_weight", "gu_own", "dn_own", "routing")


def layer(*operands):
    moves = gather_moves(PIECES)
    program = gather_program(moves, DEPTH)
    bf, wide = jnp.bfloat16, jnp.float32
    buffers = dict(
        normed=pltpu.VMEM((ROWS, MODEL_WIDTH), bf),
        pairs=pltpu.VMEM((WINDOW + ROWS, 256), bf),
        queries=pltpu.VMEM((ROWS, 384), bf),
        attended=pltpu.VMEM((ROWS, 384), bf),
        projected=pltpu.VMEM((4, PART, MODEL_WIDTH), bf),
        projected_in=pltpu.VMEM((3, PART, MODEL_WIDTH), bf),
        routing_other=pltpu.VMEM((4, 8, PART), wide),
        slots=pltpu.VMEM((4, 2, 2 * SLOTS, PART), bf),
        slot_gates=pltpu.VMEM((2, 4, PART, 1), wide),
        middle=pltpu.VMEM((PART, MODEL_WIDTH), bf),
        states=pltpu.VMEM((2, 4, PART, MODEL_WIDTH), bf),
        routed=pltpu.VMEM((2, 4, PART, MODEL_WIDTH), bf),
        hidden=pltpu.VMEM((2, 4 * PART, FF), bf),
        produced=pltpu.VMEM((2, 4, PART, N_CHUNK), bf),
        outgoing=pltpu.VMEM((2, 4, PART, MODEL_WIDTH), bf),
        core_in=pltpu.VMEM((4, PART, MODEL_WIDTH), bf),
        merged=pltpu.VMEM((4, PART, MODEL_WIDTH), bf),
        column_in=pltpu.VMEM((3, PART, MODEL_WIDTH), bf),
        gu=pltpu.VMEM((2, 16, 96, MODEL_WIDTH), bf),
        dn=pltpu.VMEM((2, 16, 48, MODEL_WIDTH), bf),
        own_sems=pltpu.SemaphoreType.DMA((2,)),
    )
    counts = dict(
        weight=len(moves), routing=1, pair=3, projected=3, state=3, across=4, core=N_CHUNKS, column=3 * N_CHUNKS
    )
    for name, count in counts.items():
        buffers[name + "_send"] = pltpu.SemaphoreType.DMA((count,))
        buffers[name + "_recv"] = pltpu.SemaphoreType.DMA((count,))
    names = INPUTS + ("out",) + tuple(buffers)

    def kernel(*refs):
        found = dict(zip(names, refs))
        for name in counts:
            found[name + "_sems"] = (found[name + "_send"], found[name + "_recv"])
        layer_kernel(moves, program, types.SimpleNamespace(**found))

    return pl.pallas_call(
        kernel,
        out_shape=jax.ShapeDtypeStruct((PART, MODEL_WIDTH), bf),
        in_specs=[pl.BlockSpec(memory_space=pltpu.VMEM)] * len(INPUTS),
        out_specs=pl.BlockSpec(memory_space=pltpu.VMEM),
        scratch_shapes=list(buffers.values()),
        compiler_params=pltpu.CompilerParams(
            collective_id=0, has_side_effects=True, vmem_limit_bytes=66_000_000
        ),
    )(*operands)


def body(
    tokens,
    segments,
    norm_gains,
    query_weight,
    key_value_matrix,
    output_weight,
    trainer_gateup,
    trainer_down,
    routes,
    route_weights,
):
    routing = jnp.concatenate(
        [routes.astype(jnp.float32).reshape(4, PART, TOPK), route_weights.reshape(4, PART, TOPK)], axis=2
    ).transpose(0, 2, 1)
    out = layer(
        tokens,
        segments.reshape(-1, 128),
        norm_gains,
        query_weight,
        key_value_matrix,
        output_weight,
        trainer_gateup[0].astype(jnp.bfloat16),
        trainer_down[0].astype(jnp.bfloat16),
        routing,
    )
    return out.reshape(1, 1, PART, MODEL_WIDTH)


def solution(mesh):
    in_specs = (
        P(("dp", "expert"), None),
        P(),
        P(),
        P(None, "mp"),
        P(),
        P("mp", None),
        P(("mp", "expert"), "dp", None),
        P(("mp", "expert"), "dp", None),
        P(("dp", "expert"), None),
        P(("dp", "expert"), None),
    )
    out_specs = P(("dp", "expert"), "mp", None, None)
    return jax.shard_map(body, mesh=mesh, in_specs=in_specs, out_specs=out_specs, check_vma=False)
```

```python
import functools
import heapq
import math
import types

import jax
import jax.numpy as jnp
from jax import lax
from jax.experimental import pallas as pl
from jax.experimental.pallas import tpu as pltpu
from jax.sharding import PartitionSpec as P

MODEL_WIDTH = 1536
FF = 768
TOPK = 4


LINKS = ("y+", "y-", "z+", "z-")
AXES = ("dp", "mp", "expert")
MESH = pl.DeviceIdType.MESH


def column_ring(moves, rank, tag, piece, halves, dy, have):
    got = {0: have}
    up, down = have, have
    for s in range(1, 4):
        moves.append(("z+", (dy, 1 - s), piece, up, (rank, tag, s)))
        up = got[-s] = [len(moves) - 1]
        moves.append(("z-", (dy, s - 1), piece, down, (rank, tag, s)))
        down = got[s] = [len(moves) - 1]
    moves.append(("z+", (dy, -3), halves[0], up, (rank, tag, 4)))
    moves.append(("z-", (dy, 3), halves[1], down, (rank, tag, 4)))
    got[4] = [len(moves) - 2, len(moves) - 1]
    return got


def row_ring(moves, rank, tag, piece, halves, dz, have, late):
    start = len(moves)
    moves.append(("y+", (0, dz), piece, have, (rank, tag, 1 + late)))
    moves.append(("y-", (0, dz), piece, have, (rank, tag, 1 + late)))
    moves.append(("y+", (-1, dz), halves[0], [start], (rank, tag, 2 + late)))
    moves.append(("y-", (1, dz), halves[1], [start + 1], (rank, tag, 2 + late)))
    return {0: have, -1: [start], 1: [start + 1], 2: [start + 2, start + 3]}


def gather_moves(pieces):
    moves = []
    for rank, order, piece, halves in pieces:
        if order == "zy":
            got = column_ring(moves, rank, 0, piece, halves, 0, [])
            for late, dz in enumerate((0, -1, 1, -2, 2, -3, 3, 4)):
                row_ring(moves, rank, 1, piece, halves, dz, got[dz], late)
        else:
            got = row_ring(moves, rank, 0, piece, halves, 0, [], 0)
            for late, dy in enumerate((0, -1, 1, 2)):
                column_ring(moves, rank, 1 + late, piece, halves, dy, got[dy])
    return moves


def gather_program(moves, rate=40e3, latency=1.7):
    issued, got = set(), set()
    free = dict.fromkeys(LINKS, 0.0)
    arrivals, now, program = [], 0.0, []
    while True:
        for link in LINKS:
            while True:
                ready = [
                    (moves[i][4], i)
                    for i in range(len(moves))
                    if moves[i][0] == link and i not in issued and got.issuperset(moves[i][3])
                ]
                if not ready:
                    break
                (rank, _, _), i = min(ready)
                if free[link] - now > (AHEAD_FIRST if rank == 0 else AHEAD):
                    break
                _, r0, r1, c0, c1 = moves[i][2]
                issued.add(i)
                program.append(("send", i, now))
                free[link] = max(now, free[link]) + (r1 - r0) * (c1 - c0) * 2 / rate
                heapq.heappush(arrivals, (free[link] + latency, i))
        if not arrivals:
            return program
        now, i = heapq.heappop(arrivals)
        got.add(i)
        program.append(("recv", i, now))


PIECES = (
    (0, "zy", ("gu", 0, 96, 0, 896), (("gu", 0, 48, 0, 896), ("gu", 48, 96, 0, 896))),
    (0, "yz", ("gu", 0, 96, 896, 1536), (("gu", 0, 48, 896, 1536), ("gu", 48, 96, 896, 1536))),
    (1, "zy", ("dn", 0, 48, 0, 256), (("dn", 0, 48, 0, 128), ("dn", 0, 48, 128, 256))),
    (1, "yz", ("dn", 0, 48, 256, 512), (("dn", 0, 48, 256, 384), ("dn", 0, 48, 384, 512))),
    (2, "zy", ("dn", 0, 48, 512, 1024), (("dn", 0, 48, 512, 768), ("dn", 0, 48, 768, 1024))),
    (3, "zy", ("dn", 0, 48, 1024, 1280), (("dn", 0, 48, 1024, 1152), ("dn", 0, 48, 1152, 1280))),
    (3, "yz", ("dn", 0, 48, 1280, 1536), (("dn", 0, 48, 1280, 1408), ("dn", 0, 48, 1408, 1536))),
)
AHEAD_FIRST = 30.0
AHEAD = 12.0
PUMP = {
    "start": 0.1, "pairs": 5.2, "query": 7.8, "onward": 15.6, "window": 23.4,
    "a00": 24.7, "a01": 26, "a02": 27.3, "a10": 28.6, "a11": 29.9, "a12": 31.2, "a20": 32.5, "a21": 33.8, "a22": 35.1,
    "project": 37.7, "slots": 41.6, "partial": 52, "middle": 55.9,
    "g0": 58.5, "g1": 63.7, "g2": 68.9, "g3": 72.8,
}

ROWS = 384
PART = 96
SLOTS = 48
WINDOW = 1152
F_CHUNK = 256
N_CHUNK = 512
N_CHUNKS = MODEL_WIDTH // N_CHUNK


def dot(a, b):
    return jnp.dot(a, b, preferred_element_type=jnp.float32)


def layer_kernel(moves, program, refs):
    r = refs
    dp, mp, expert = (lax.axis_index(a) for a in AXES)
    y, z_lo, z_hi, core = dp // 4, dp % 4, expert // 2, expert % 2
    z = z_hi * 4 + z_lo
    group = dp * 4 + expert

    def place(dy, dz):
        other_y, other_z = (y + dy + 8) % 4, (z + dz + 8) % 8
        return other_z // 4, other_y * 4 + other_z % 4

    def grid_device(dy, dz):
        half, index = place(dy, dz)
        return (index, mp, half * 2 + core)

    def column_device(d):
        return (dp, (mp + d + 4) % 4, expert)

    def piece_device(d):
        other = (group + d + 64) % 64
        return (other // 4, mp, other % 4)

    partner = (dp, mp, z_hi * 2 + 1 - core)
    target = {"y+": (1, 0), "y-": (-1, 0), "z+": (0, 1), "z-": (0, -1)}

    barrier = pltpu.get_barrier_semaphore()
    greeted = [grid_device(*target[link]) for link in LINKS]
    beside = (dp, mp + 1 - 2 * (mp % 2), expert)
    across = (dp, mp + 1 - 2 * (mp % 2), z_hi * 2 + 1 - core)
    greeted += [column_device(d) for d in (1, 2, 3)] + [partner, across]
    greeted += [piece_device(-2), piece_device(2 * core - 3)]
    for other in greeted:
        pl.semaphore_signal(barrier, inc=1, device_id=other, device_id_type=MESH)
    sent = []

    class Transfer:
        def __init__(self, start, landing, sems, i, device):
            self.copy = pltpu.make_async_remote_copy(
                src_ref=start,
                dst_ref=landing,
                send_sem=sems[0].at[i],
                recv_sem=sems[1].at[i],
                device_id=device,
                device_id_type=MESH,
            )

        def start(self):
            self.copy.start()
            sent.append(self)

        def wait_recv(self):
            self.copy.wait_recv()

    remote = Transfer

    whole = {"gu": r.gu, "dn": r.dn}

    def weight_copy(i):
        link, (dy, dz), (name, r0, r1, c0, c1), _, _ = moves[i]
        half, index = place(dy, dz)
        slab = whole[name].at[half, index, pl.ds(r0, r1 - r0), pl.ds(c0, c1 - c0)]
        return remote(slab, slab, r.weight_sems, i, grid_device(*target[link]))

    position = [0]

    def advance(stop):
        while position[0] < len(program) and not stop(program[position[0]]):
            kind, i, _ = program[position[0]]
            if kind == "send":
                weight_copy(i).start()
            else:
                weight_copy(i).wait_recv()
            position[0] += 1

    def pump(name):
        advance(lambda step: step[2] > PUMP[name])

    def pump_for(span):
        if position[0] < len(program):
            end = program[position[0]][2] + span
            advance(lambda step: step[2] > end)

    def have(name, columns):
        needed = {
            i for i, move in enumerate(moves)
            if move[2][0] == name and move[2][3] < columns[1] and columns[0] < move[2][4]
        }
        needed -= {i for kind, i, _ in program[: position[0]] if kind == "recv"}

        def stop(step):
            if not needed:
                return True
            if step[0] == "recv":
                needed.discard(step[1])
            return False

        advance(stop)

    half, index = place(0, 0)
    arriving = {}
    for k, name in enumerate(LOADED):
        start = getattr(r, name)
        if name == "pair_weight":
            start = start.at[mp // 2]
        arriving[name] = pltpu.make_async_copy(start, getattr(r, name + "_here"), r.load_sems.at[k])
        arriving[name].start()
    arriving["trainer_gateup"].wait()
    r.gu[half, index] = r.trainer_gateup_here[...].astype(jnp.bfloat16)
    arriving["trainer_down"].wait()
    r.dn[half, index] = r.trainer_down_here[...].astype(jnp.bfloat16)
    barrier = pltpu.get_barrier_semaphore()
    pl.semaphore_wait(barrier, len(greeted))
    routing = [
        remote(here, there, r.routing_sems, k, partner)
        for k, (here, there) in enumerate(((r.routes, r.routes_other), (r.gates, r.gates_other)))
    ]
    for copy in routing:
        copy.start()
    pump("start")

    arriving["tokens"].wait()
    gain = r.gains[0:1, :]

    @pl.loop(0, ROWS // 32)
    def _(i):
        rows = pl.ds(pl.multiple_of(i * 32, 32), 32)
        wide = r.tokens_here[rows, :].astype(jnp.float32)
        scale = lax.rsqrt(jnp.mean(wide * wide, axis=-1, keepdims=True) + 1e-6)
        r.normed[rows, :] = (wide * scale * gain).astype(jnp.bfloat16)

    arriving["pair_weight"].wait()
    pair = dot(r.normed[...], r.pair_weight_here[...]).astype(jnp.bfloat16)
    for part in range(2):
        r.pairs[part, WINDOW:, :] = pair[:, part * 128 : (part + 1) * 128]

    half_here = mp % 2

    def piece_rows(k):
        return pl.ds(pl.multiple_of(k * ROWS, ROWS), ROWS)

    onward = remote(
        r.pairs.at[half_here, piece_rows(3)], r.pairs.at[half_here, piece_rows(1)], r.pair_sems, 0, piece_device(2)
    )
    direct = remote(
        r.pairs.at[:, piece_rows(3)],
        r.pairs.at[:, piece_rows(2 - 2 * core)],
        r.pair_sems,
        1,
        piece_device(1 + 2 * core),
    )
    landed = r.pairs.at[half_here, piece_rows(1)]
    crossing = r.pairs.at[half_here, piece_rows(2 * core)]
    shares = [
        remote(landed, landed, r.pair_sems, 2, beside),
        remote(landed, crossing, r.pair_sems, 3, partner),
        remote(landed, crossing, r.pair_sems, 4, across),
    ]
    onward.start()
    direct.start()
    pump("pairs")
    arriving["query_weight"].wait()
    r.queries[...] = dot(r.normed[...], r.query_weight_here[...]).astype(jnp.bfloat16)
    pump("query")

    lanes = []
    for k in range(12):
        row = (group * 3 - 9 + k + 192) % 192
        lanes.append(r.segments[pl.ds(row, 1), :])
    key_segment = jnp.concatenate(lanes, axis=1)
    diagonal = lax.broadcasted_iota(jnp.int32, (128, 128), 0) == lax.broadcasted_iota(
        jnp.int32, (128, 128), 1
    )
    first_key = (group - 3) * ROWS

    pump("onward")
    onward.wait_recv()
    for copy in shares:
        copy.start()
    pump("window")
    for copy in shares + [direct]:
        copy.wait_recv()
    for c in range(3):
        low = (c + 1) * 128
        own_lanes = jnp.broadcast_to(lanes[9 + c].astype(jnp.float32), (128, 128))
        query_segment = jnp.sum(jnp.where(diagonal, own_lanes, 0.0), axis=1, keepdims=True)
        key_offset = low + lax.broadcasted_iota(jnp.int32, (128, WINDOW), 1)
        query_offset = WINDOW + c * 128 + lax.broadcasted_iota(jnp.int32, (128, WINDOW), 0)
        allowed = (
            (key_segment[:, low : low + WINDOW].astype(jnp.float32) == query_segment)
            & (key_offset <= query_offset)
            & (key_offset + first_key >= 0)
        )
        keys = r.pairs[0, low : low + WINDOW, :]
        values = r.pairs[1, low : low + WINDOW, :]
        for h in range(3):
            query = r.queries[c * 128 : (c + 1) * 128, h * 128 : (h + 1) * 128]
            scores = lax.dot_general(
                query, keys, (((1,), (1,)), ((), ())), preferred_element_type=jnp.float32
            )
            scores = jnp.where(allowed, scores * (1.0 / math.sqrt(128)), -1e30)
            weights = jnp.exp(scores - jnp.max(scores, axis=1, keepdims=True))
            total = jnp.sum(weights, axis=1, keepdims=True)
            mixed = dot(weights.astype(jnp.bfloat16), values) / total
            r.attended[c * 128 : (c + 1) * 128, h * 128 : (h + 1) * 128] = mixed.astype(jnp.bfloat16)
            pump(f"a{c}{h}")

    def partial_copy(d):
        return remote(
            r.projected.at[(mp + d) % 4], r.projected_in.at[d - 1], r.projected_sems, d - 1, column_device(d)
        )

    arriving["output_weight"].wait()
    r.projected[...] = (
        dot(r.attended[...], r.output_weight_here[...]).astype(jnp.bfloat16).reshape(4, PART, MODEL_WIDTH)
    )
    for d in (2, 1, 3):
        partial_copy(d).start()
    pump("project")

    for copy in routing:
        copy.wait_recv()
    before = lax.broadcasted_iota(jnp.int32, (ROWS, ROWS), 0)
    token = lax.broadcasted_iota(jnp.int32, (ROWS, ROWS), 1)
    earlier = ((before < token) & (before // PART == token // PART)).astype(jnp.bfloat16)
    slot = lax.broadcasted_iota(jnp.int32, (SLOTS, ROWS), 0).astype(jnp.float32)
    for side, (routes, gates) in enumerate(((r.routes, r.gates), (r.routes_other, r.gates_other))):
        for e in range(2):
            named = routes[...] == mp * 4 + e * 2 + core
            hit = jnp.sum(jnp.where(named, 1.0, 0.0), axis=0, keepdims=True)
            gate = jnp.sum(jnp.where(named, gates[...], 0.0), axis=0, keepdims=True)
            rank = dot(jnp.broadcast_to(hit, (8, ROWS)).astype(jnp.bfloat16), earlier)[0:1, :]
            chosen = jnp.where((slot == rank) & (hit > 0.5), 1.0, 0.0)
            weighed = chosen * gate
            for m in range(4):
                lanes = slice(m * PART, (m + 1) * PART)
                r.slots[m, side, e * SLOTS : (e + 1) * SLOTS, :] = chosen[:, lanes].astype(jnp.bfloat16)
                r.slot_gates[e, m, side * SLOTS : (side + 1) * SLOTS, :] = jnp.sum(
                    weighed[:, lanes], axis=1, keepdims=True
                )
    pump("slots")
    pump("partial")

    for d in (1, 2, 3):
        partial_copy(d).wait_recv()
    summed = r.tokens_here[pl.ds(pl.multiple_of(mp * PART, PART), PART), :].astype(jnp.float32)
    attention = r.projected[mp].astype(jnp.float32)
    for d in range(3):
        attention = attention + r.projected_in[d].astype(jnp.float32)
    middle = (summed + attention).astype(jnp.bfloat16)
    r.middle[...] = middle
    wide = middle.astype(jnp.float32)
    scale = lax.rsqrt(jnp.mean(wide * wide, axis=-1, keepdims=True) + 1e-6)
    r.states[0, 0] = (wide * scale * r.gains[1:2, :]).astype(jnp.bfloat16)

    def state_copy(d):
        return remote(r.states.at[0, 0], r.states.at[0, d], r.state_sems, d - 1, column_device(d))

    def across_copy(d):
        return remote(r.states.at[0, d], r.states.at[1, d], r.across_sems, d, partner)

    for d in (2, 1, 3):
        state_copy(d).start()
    across_copy(0).start()
    pump("middle")
    for step, d in enumerate((0, 1, 3, 2)):
        pump(f"g{step}")
        if d:
            state_copy(d).wait_recv()
            across_copy(d).start()
        for side in range(2):
            if side:
                across_copy(d).wait_recv()
            picked = dot(r.slots[(mp - d + 4) % 4, side], r.states[side, d]).astype(jnp.bfloat16)
            for e in range(2):
                r.routed[e, d, side * SLOTS : (side + 1) * SLOTS, :] = picked[e * SLOTS : (e + 1) * SLOTS]

    have("gu", (0, MODEL_WIDTH))
    for e in range(2):
        inputs = r.routed[e].reshape(4 * PART, MODEL_WIDTH)
        for f in range(3):
            left = f * F_CHUNK
            gate = dot(inputs, r.gu[e, :, :, left : left + F_CHUNK].reshape(MODEL_WIDTH, F_CHUNK))
            rise = dot(inputs, r.gu[e, :, :, FF + left : FF + left + F_CHUNK].reshape(MODEL_WIDTH, F_CHUNK))
            r.hidden[e, :, left : left + F_CHUNK] = (jnp.maximum(gate, 0.0) * rise).astype(jnp.bfloat16)
            pump_for(0.7)

    def return_core(n):
        columns = pl.ds(n * N_CHUNK, N_CHUNK)
        return remote(
            r.outgoing.at[1, :, :, columns], r.core_in.at[:, :, columns], r.core_sems, n, partner
        )

    def return_column(n, d):
        columns = pl.ds(n * N_CHUNK, N_CHUNK)
        return remote(
            r.merged.at[d, :, columns],
            r.column_in.at[d - 1, :, columns],
            r.column_sems,
            n * 3 + d - 1,
            column_device(-d),
        )

    def merge(n):
        columns = slice(n * N_CHUNK, (n + 1) * N_CHUNK)
        return_core(n).wait_recv()
        for d in (2, 1, 3, 0):
            both = r.outgoing[0, d, :, columns].astype(jnp.float32) + r.core_in[d, :, columns].astype(
                jnp.float32
            )
            r.merged[d, :, columns] = both.astype(jnp.bfloat16)
        for d in (2, 1, 3):
            return_column(n, d).start()

    for n in range(N_CHUNKS):
        columns = slice(n * N_CHUNK, (n + 1) * N_CHUNK)
        have("dn", (n * N_CHUNK, (n + 1) * N_CHUNK))
        for e in range(2):
            produced = dot(r.hidden[e], r.dn[e, :, :, columns].reshape(FF, N_CHUNK))
            for d in range(4):
                rows = produced[d * PART : (d + 1) * PART] * r.slot_gates[e, (mp - d + 4) % 4]
                r.produced[e, d] = rows.astype(jnp.bfloat16)
            pump_for(0.8)
        for side in (1, 0):
            for d in range(4):
                rows = slice(side * SLOTS, (side + 1) * SLOTS)
                stacked = jnp.concatenate([r.produced[0, d, rows, :], r.produced[1, d, rows, :]], axis=0)
                back = lax.dot_general(
                    r.slots[(mp - d + 4) % 4, side], stacked, (((0,), (0,)), ((), ())), preferred_element_type=jnp.float32
                )
                r.outgoing[side, d, :, columns] = back.astype(jnp.bfloat16)
            if side:
                return_core(n).start()
            pump_for(0.8)
        if n:
            merge(n - 1)
    merge(N_CHUNKS - 1)
    for n in range(N_CHUNKS):
        columns = slice(n * N_CHUNK, (n + 1) * N_CHUNK)
        for d in (1, 2, 3):
            return_column(n, d).wait_recv()
        result = r.middle[:, columns].astype(jnp.float32) + r.merged[0, :, columns].astype(jnp.float32)
        for d in range(3):
            result = result + r.column_in[d, :, columns].astype(jnp.float32)
        r.out[:, columns] = result.astype(jnp.bfloat16)

    for copy in sent:
        copy.copy.wait_send()


LOADED = ("trainer_gateup", "trainer_down", "tokens", "pair_weight", "query_weight", "output_weight")
INPUTS = LOADED + ("segments", "gains", "routes", "gates")


def layer(*operands):
    moves = gather_moves(PIECES)
    program = gather_program(moves)
    bf, wide = jnp.bfloat16, jnp.float32
    buffers = dict(
        normed=pltpu.VMEM((ROWS, MODEL_WIDTH), bf),
        pairs=pltpu.VMEM((2, WINDOW + ROWS, 128), bf),
        queries=pltpu.VMEM((ROWS, 384), bf),
        attended=pltpu.VMEM((ROWS, 384), bf),
        projected=pltpu.VMEM((4, PART, MODEL_WIDTH), bf),
        projected_in=pltpu.VMEM((3, PART, MODEL_WIDTH), bf),
        routes_other=pltpu.VMEM((TOPK, ROWS), jnp.int32),
        gates_other=pltpu.VMEM((TOPK, ROWS), wide),
        slots=pltpu.VMEM((4, 2, 2 * SLOTS, PART), bf),
        slot_gates=pltpu.VMEM((2, 4, PART, 1), wide),
        middle=pltpu.VMEM((PART, MODEL_WIDTH), bf),
        states=pltpu.VMEM((2, 4, PART, MODEL_WIDTH), bf),
        routed=pltpu.VMEM((2, 4, PART, MODEL_WIDTH), bf),
        hidden=pltpu.VMEM((2, 4 * PART, FF), bf),
        produced=pltpu.VMEM((2, 4, PART, N_CHUNK), bf),
        outgoing=pltpu.VMEM((2, 4, PART, MODEL_WIDTH), bf),
        core_in=pltpu.VMEM((4, PART, MODEL_WIDTH), bf),
        merged=pltpu.VMEM((4, PART, MODEL_WIDTH), bf),
        column_in=pltpu.VMEM((3, PART, MODEL_WIDTH), bf),
        gu=pltpu.VMEM((2, 16, 96, MODEL_WIDTH), bf),
        dn=pltpu.VMEM((2, 16, 48, MODEL_WIDTH), bf),
        load_sems=pltpu.SemaphoreType.DMA((len(LOADED),)),
    )
    for name, operand in zip(LOADED, operands):
        shape = operand.shape[1:] if name == "pair_weight" else operand.shape
        buffers[name + "_here"] = pltpu.VMEM(shape, operand.dtype)
    counts = dict(
        weight=len(moves), routing=2, pair=5, projected=3, state=3, across=4, core=N_CHUNKS, column=3 * N_CHUNKS
    )
    for name, count in counts.items():
        buffers[name + "_send"] = pltpu.SemaphoreType.DMA((count,))
        buffers[name + "_recv"] = pltpu.SemaphoreType.DMA((count,))
    names = INPUTS + ("out",) + tuple(buffers)

    def kernel(*refs):
        found = dict(zip(names, refs))
        for name in counts:
            found[name + "_sems"] = (found[name + "_send"], found[name + "_recv"])
        layer_kernel(moves, program, types.SimpleNamespace(**found))

    return pl.pallas_call(
        kernel,
        out_shape=jax.ShapeDtypeStruct((PART, MODEL_WIDTH), bf),
        in_specs=[
            pl.BlockSpec(memory_space=pl.ANY if name in LOADED else pltpu.VMEM) for name in INPUTS
        ],
        out_specs=pl.BlockSpec(memory_space=pltpu.VMEM),
        scratch_shapes=list(buffers.values()),
        compiler_params=pltpu.CompilerParams(
            collective_id=0, has_side_effects=True, vmem_limit_bytes=66_000_000
        ),
    )(*operands)


def body(
    tokens,
    segments,
    norm_gains,
    query_weight,
    key_value_matrix,
    output_weight,
    trainer_gateup,
    trainer_down,
    routes,
    route_weights,
):
    out = layer(
        trainer_gateup[0],
        trainer_down[0],
        tokens,
        key_value_matrix,
        query_weight,
        output_weight,
        segments.reshape(-1, 128),
        norm_gains,
        routes.T,
        route_weights.T,
    )
    return out.reshape(1, 1, PART, MODEL_WIDTH)


def solution(mesh):
    in_specs = (
        P(("dp", "expert"), None),
        P(),
        P(),
        P(None, "mp"),
        P(),
        P("mp", None),
        P(("mp", "expert"), "dp", None),
        P(("mp", "expert"), "dp", None),
        P(("dp", "expert"), None),
        P(("dp", "expert"), None),
    )
    out_specs = P(("dp", "expert"), "mp", None, None)
    return jax.shard_map(body, mesh=mesh, in_specs=in_specs, out_specs=out_specs, check_vma=False)
```

```python
import functools
import heapq
import math
import types

import jax
import jax.numpy as jnp
from jax import lax
from jax.experimental import pallas as pl
from jax.experimental.pallas import tpu as pltpu
from jax.sharding import PartitionSpec as P

MODEL_WIDTH = 1536
FF = 768
TOPK = 4


LINKS = ("y+", "y-", "z+", "z-")
AXES = ("dp", "mp", "expert")
MESH = pl.DeviceIdType.MESH


def column_ring(moves, rank, tag, piece, halves, dy, have):
    got = {0: have}
    up, down = have, have
    for s in range(1, 4):
        moves.append(("z+", (dy, 1 - s), piece, up, (rank, tag, s)))
        up = got[-s] = [len(moves) - 1]
        moves.append(("z-", (dy, s - 1), piece, down, (rank, tag, s)))
        down = got[s] = [len(moves) - 1]
    moves.append(("z+", (dy, -3), halves[0], up, (rank, tag, 4)))
    moves.append(("z-", (dy, 3), halves[1], down, (rank, tag, 4)))
    got[4] = [len(moves) - 2, len(moves) - 1]
    return got


def row_ring(moves, rank, tag, piece, halves, dz, have, late):
    start = len(moves)
    moves.append(("y+", (0, dz), piece, have, (rank, tag, 1 + late)))
    moves.append(("y-", (0, dz), piece, have, (rank, tag, 1 + late)))
    moves.append(("y+", (-1, dz), halves[0], [start], (rank, tag, 2 + late)))
    moves.append(("y-", (1, dz), halves[1], [start + 1], (rank, tag, 2 + late)))
    return {0: have, -1: [start], 1: [start + 1], 2: [start + 2, start + 3]}


def gather_moves(pieces):
    moves = []
    for rank, order, piece, halves in pieces:
        if order == "zy":
            got = column_ring(moves, rank, 0, piece, halves, 0, [])
            for late, dz in enumerate((0, -1, 1, -2, 2, -3, 3, 4)):
                row_ring(moves, rank, 1, piece, halves, dz, got[dz], late)
        else:
            got = row_ring(moves, rank, 0, piece, halves, 0, [], 0)
            for late, dy in enumerate((0, -1, 1, 2)):
                column_ring(moves, rank, 1 + late, piece, halves, dy, got[dy])
    return moves


def gather_program(moves, rate=40e3, latency=1.7):
    issued, got = set(), set()
    free = dict.fromkeys(LINKS, 0.0)
    arrivals, now, program = [], 0.0, []
    while True:
        for link in LINKS:
            while True:
                ready = [
                    (moves[i][4], i)
                    for i in range(len(moves))
                    if moves[i][0] == link and i not in issued and got.issuperset(moves[i][3])
                ]
                if not ready:
                    break
                (rank, _, _), i = min(ready)
                if free[link] - now > (AHEAD_FIRST if rank == 0 else AHEAD):
                    break
                _, r0, r1, c0, c1 = moves[i][2]
                issued.add(i)
                program.append(("send", i, now))
                free[link] = max(now, free[link]) + (r1 - r0) * (c1 - c0) * 2 / rate
                heapq.heappush(arrivals, (free[link] + latency, i))
        if not arrivals:
            return program
        now, i = heapq.heappop(arrivals)
        got.add(i)
        program.append(("recv", i, now))


PIECES = (
    (0, "zy", ("gu", 0, 64, 0, 1536), (("gu", 0, 32, 0, 1536), ("gu", 32, 64, 0, 1536))),
    (0, "yz", ("gu", 64, 96, 0, 1536), (("gu", 64, 80, 0, 1536), ("gu", 80, 96, 0, 1536))),
    (1, "zy", ("dn", 0, 48, 0, 768), (("dn", 0, 48, 0, 384), ("dn", 0, 48, 384, 768))),
    (1, "yz", ("dn", 0, 48, 768, 1536), (("dn", 0, 48, 768, 1152), ("dn", 0, 48, 1152, 1536))),
)
AHEAD_FIRST = 30.0
AHEAD = 12.0
PUMP = {
    "start": 0.1, "pairs": 4.4, "query": 6.6, "onward": 13.3, "window": 19.9,
    "a00": 21.0, "a01": 22.1, "a02": 23.2, "a10": 24.3, "a11": 25.4, "a12": 26.5, "a20": 27.6, "a21": 28.7, "a22": 29.8,
    "project": 32.0, "slots": 35.4, "partial": 44.2, "middle": 47.5,
    "g0": 49.7, "g1": 60.5, "g2": 65.5, "g3": 69.2,
}

ROWS = 384
PART = 96
SLOTS = 48
WINDOW = 1152
F_CHUNK = 256
BLOCKS = ((0, 512), (512, 896), (896, 1280), (1280, 1536))


def dot(a, b):
    return jnp.dot(a, b, preferred_element_type=jnp.float32)


def layer_kernel(moves, program, refs):
    r = refs
    dp, mp, expert = (lax.axis_index(a) for a in AXES)
    y, z_lo, z_hi, core = dp // 4, dp % 4, expert // 2, expert % 2
    z = z_hi * 4 + z_lo
    group = dp * 4 + expert

    def place(dy, dz):
        other_y, other_z = (y + dy + 8) % 4, (z + dz + 8) % 8
        return other_z // 4, other_y * 4 + other_z % 4

    def grid_device(dy, dz):
        half, index = place(dy, dz)
        return (index, mp, half * 2 + core)

    def column_device(d):
        return (dp, (mp + d + 4) % 4, expert)

    def piece_device(d):
        other = (group + d + 64) % 64
        return (other // 4, mp, other % 4)

    partner = (dp, mp, z_hi * 2 + 1 - core)
    target = {"y+": (1, 0), "y-": (-1, 0), "z+": (0, 1), "z-": (0, -1)}

    barrier = pltpu.get_barrier_semaphore()
    greeted = [grid_device(*target[link]) for link in LINKS]
    beside = (dp, mp + 1 - 2 * (mp % 2), expert)
    across = (dp, mp + 1 - 2 * (mp % 2), z_hi * 2 + 1 - core)
    greeted += [column_device(d) for d in (1, 2, 3)] + [partner, across]
    greeted += [piece_device(-2), piece_device(2 * core - 3)]
    for other in greeted:
        pl.semaphore_signal(barrier, inc=1, device_id=other, device_id_type=MESH)
    sent = []

    class Transfer:
        def __init__(self, start, landing, sems, i, device):
            self.copy = pltpu.make_async_remote_copy(
                src_ref=start,
                dst_ref=landing,
                send_sem=sems[0].at[i],
                recv_sem=sems[1].at[i],
                device_id=device,
                device_id_type=MESH,
            )

        def start(self):
            self.copy.start()
            sent.append(self)

        def wait_recv(self):
            self.copy.wait_recv()

    remote = Transfer

    whole = {"gu": r.gu, "dn": r.dn}

    def weight_copy(i):
        link, (dy, dz), (name, r0, r1, c0, c1), _, _ = moves[i]
        half, index = place(dy, dz)
        slab = whole[name].at[half, index, pl.ds(r0, r1 - r0), pl.ds(c0, c1 - c0)]
        return remote(slab, slab, r.weight_sems, i, grid_device(*target[link]))

    position = [0]

    def advance(stop):
        while position[0] < len(program) and not stop(program[position[0]]):
            kind, i, _ = program[position[0]]
            if kind == "send":
                weight_copy(i).start()
            else:
                weight_copy(i).wait_recv()
            position[0] += 1

    def pump(name):
        advance(lambda step: step[2] > PUMP[name])

    def pump_for(span):
        if position[0] < len(program):
            end = program[position[0]][2] + span
            advance(lambda step: step[2] > end)

    def have(name, columns):
        needed = {
            i for i, move in enumerate(moves)
            if move[2][0] == name and move[2][3] < columns[1] and columns[0] < move[2][4]
        }
        needed -= {i for kind, i, _ in program[: position[0]] if kind == "recv"}

        def stop(step):
            if not needed:
                return True
            if step[0] == "recv":
                needed.discard(step[1])
            return False

        advance(stop)

    half, index = place(0, 0)
    arriving = {}
    for k, name in enumerate(LOADED):
        start = getattr(r, name)
        if name == "pair_weight":
            start = start.at[mp // 2]
        arriving[name] = pltpu.make_async_copy(start, getattr(r, name + "_here"), r.load_sems.at[k])
        arriving[name].start()
    arriving["trainer_gateup"].wait()
    r.gu[half, index] = r.trainer_gateup_here[...].astype(jnp.bfloat16)
    arriving["trainer_down"].wait()
    r.dn[half, index] = r.trainer_down_here[...].astype(jnp.bfloat16)
    barrier = pltpu.get_barrier_semaphore()
    pl.semaphore_wait(barrier, len(greeted))
    routing = [
        remote(here, there, r.routing_sems, k, partner)
        for k, (here, there) in enumerate(((r.routes, r.routes_other), (r.gates, r.gates_other)))
    ]
    for copy in routing:
        copy.start()
    pump("start")

    arriving["tokens"].wait()
    gain = r.gains[0:1, :]

    @pl.loop(0, ROWS // 32)
    def _(i):
        rows = pl.ds(pl.multiple_of(i * 32, 32), 32)
        wide = r.tokens_here[rows, :].astype(jnp.float32)
        scale = lax.rsqrt(jnp.mean(wide * wide, axis=-1, keepdims=True) + 1e-6)
        r.normed[rows, :] = (wide * scale * gain).astype(jnp.bfloat16)

    arriving["pair_weight"].wait()
    pair = dot(r.normed[...], r.pair_weight_here[...]).astype(jnp.bfloat16)
    for part in range(2):
        r.pairs[part, WINDOW:, :] = pair[:, part * 128 : (part + 1) * 128]

    half_here = mp % 2

    def piece_rows(k):
        return pl.ds(pl.multiple_of(k * ROWS, ROWS), ROWS)

    onward = remote(
        r.pairs.at[half_here, piece_rows(3)], r.pairs.at[half_here, piece_rows(1)], r.pair_sems, 0, piece_device(2)
    )
    direct = remote(
        r.pairs.at[:, piece_rows(3)],
        r.pairs.at[:, piece_rows(2 - 2 * core)],
        r.pair_sems,
        1,
        piece_device(1 + 2 * core),
    )
    landed = r.pairs.at[half_here, piece_rows(1)]
    crossing = r.pairs.at[half_here, piece_rows(2 * core)]
    shares = [
        remote(landed, landed, r.pair_sems, 2, beside),
        remote(landed, crossing, r.pair_sems, 3, partner),
        remote(landed, crossing, r.pair_sems, 4, across),
    ]
    onward.start()
    direct.start()
    pump("pairs")
    arriving["query_weight"].wait()
    r.queries[...] = dot(r.normed[...], r.query_weight_here[...]).astype(jnp.bfloat16)
    pump("query")

    lanes = []
    for k in range(12):
        row = (group * 3 - 9 + k + 192) % 192
        lanes.append(r.segments[pl.ds(row, 1), :])
    key_segment = jnp.concatenate(lanes, axis=1)
    diagonal = lax.broadcasted_iota(jnp.int32, (128, 128), 0) == lax.broadcasted_iota(
        jnp.int32, (128, 128), 1
    )
    first_key = (group - 3) * ROWS

    pump("onward")
    onward.wait_recv()
    for copy in shares:
        copy.start()
    pump("window")
    for copy in shares + [direct]:
        copy.wait_recv()
    for c in range(3):
        low = (c + 1) * 128
        own_lanes = jnp.broadcast_to(lanes[9 + c].astype(jnp.float32), (128, 128))
        query_segment = jnp.sum(jnp.where(diagonal, own_lanes, 0.0), axis=1, keepdims=True)
        key_offset = low + lax.broadcasted_iota(jnp.int32, (128, WINDOW), 1)
        query_offset = WINDOW + c * 128 + lax.broadcasted_iota(jnp.int32, (128, WINDOW), 0)
        allowed = (
            (key_segment[:, low : low + WINDOW].astype(jnp.float32) == query_segment)
            & (key_offset <= query_offset)
            & (key_offset + first_key >= 0)
        )
        keys = r.pairs[0, low : low + WINDOW, :]
        values = r.pairs[1, low : low + WINDOW, :]
        for h in range(3):
            query = r.queries[c * 128 : (c + 1) * 128, h * 128 : (h + 1) * 128]
            scores = lax.dot_general(
                query, keys, (((1,), (1,)), ((), ())), preferred_element_type=jnp.float32
            )
            scores = jnp.where(allowed, scores * (1.0 / math.sqrt(128)), -1e30)
            weights = jnp.exp(scores - jnp.max(scores, axis=1, keepdims=True))
            total = jnp.sum(weights, axis=1, keepdims=True)
            mixed = dot(weights.astype(jnp.bfloat16), values) / total
            r.attended[c * 128 : (c + 1) * 128, h * 128 : (h + 1) * 128] = mixed.astype(jnp.bfloat16)
            pump(f"a{c}{h}")

    def partial_copy(d):
        return remote(
            r.projected.at[(mp + d) % 4], r.projected_in.at[d - 1], r.projected_sems, d - 1, column_device(d)
        )

    arriving["output_weight"].wait()
    r.projected[...] = (
        dot(r.attended[...], r.output_weight_here[...]).astype(jnp.bfloat16).reshape(4, PART, MODEL_WIDTH)
    )
    for d in (2, 1, 3):
        partial_copy(d).start()
    pump("project")

    for copy in routing:
        copy.wait_recv()
    before = lax.broadcasted_iota(jnp.int32, (ROWS, ROWS), 0)
    token = lax.broadcasted_iota(jnp.int32, (ROWS, ROWS), 1)
    earlier = ((before < token) & (before // PART == token // PART)).astype(jnp.bfloat16)
    slot = lax.broadcasted_iota(jnp.int32, (SLOTS, ROWS), 0).astype(jnp.float32)
    for side, (routes, gates) in enumerate(((r.routes, r.gates), (r.routes_other, r.gates_other))):
        picks = []
        for e in range(2):
            named = routes[...] == mp * 4 + e * 2 + core
            hit = jnp.sum(jnp.where(named, 1.0, 0.0), axis=0, keepdims=True)
            gate = jnp.sum(jnp.where(named, gates[...], 0.0), axis=0, keepdims=True)
            rank = dot(jnp.broadcast_to(hit, (8, ROWS)).astype(jnp.bfloat16), earlier)[0:1, :]
            chosen = jnp.where((slot == rank) & (hit > 0.5), 1.0, 0.0)
            picks.append(chosen)
            weighed = chosen * gate
            for m in range(4):
                lanes = slice(m * PART, (m + 1) * PART)
                r.slots[m, side, e * SLOTS : (e + 1) * SLOTS, :] = chosen[:, lanes].astype(jnp.bfloat16)
                r.slot_gates[e, m, side * SLOTS : (side + 1) * SLOTS, :] = jnp.sum(
                    weighed[:, lanes], axis=1, keepdims=True
                )
        for m in range(4):
            both = jnp.concatenate([chosen[:, m * PART : (m + 1) * PART] for chosen in picks], axis=0)
            r.slots_back[m, side] = both.T.astype(jnp.bfloat16)
    pump("slots")
    pump("partial")

    for d in (1, 2, 3):
        partial_copy(d).wait_recv()
    summed = r.tokens_here[pl.ds(pl.multiple_of(mp * PART, PART), PART), :].astype(jnp.float32)
    attention = r.projected[mp].astype(jnp.float32)
    for d in range(3):
        attention = attention + r.projected_in[d].astype(jnp.float32)
    middle = (summed + attention).astype(jnp.bfloat16)
    r.middle[...] = middle
    wide = middle.astype(jnp.float32)
    scale = lax.rsqrt(jnp.mean(wide * wide, axis=-1, keepdims=True) + 1e-6)
    r.states[0, 0] = (wide * scale * r.gains[1:2, :]).astype(jnp.bfloat16)

    def state_copy(d):
        return remote(r.states.at[0, 0], r.states.at[0, d], r.state_sems, d - 1, column_device(d))

    def across_copy(d):
        return remote(r.states.at[0, d], r.states.at[1, d], r.across_sems, d, partner)

    for d in (2, 1, 3):
        state_copy(d).start()
    across_copy(0).start()
    pump("middle")
    for step, d in enumerate((0, 1, 3, 2)):
        pump(f"g{step}")
        if d:
            state_copy(d).wait_recv()
            across_copy(d).start()
        for side in range(2):
            if side:
                across_copy(d).wait_recv()
            picked = dot(r.slots[(mp - d + 4) % 4, side], r.states[side, d]).astype(jnp.bfloat16)
            for e in range(2):
                r.routed[e, d, side * SLOTS : (side + 1) * SLOTS, :] = picked[e * SLOTS : (e + 1) * SLOTS]

    have("gu", (0, MODEL_WIDTH))
    for e in range(2):
        inputs = r.routed[e].reshape(4 * PART, MODEL_WIDTH)
        for f in range(3):
            left = f * F_CHUNK
            gate = dot(inputs, r.gu[e, :, :, left : left + F_CHUNK].reshape(MODEL_WIDTH, F_CHUNK))
            rise = dot(inputs, r.gu[e, :, :, FF + left : FF + left + F_CHUNK].reshape(MODEL_WIDTH, F_CHUNK))
            r.hidden[e, :, left : left + F_CHUNK] = (jnp.maximum(gate, 0.0) * rise).astype(jnp.bfloat16)
            pump_for(0.7)

    def return_core(n):
        columns = pl.ds(BLOCKS[n][0], BLOCKS[n][1] - BLOCKS[n][0])
        return remote(
            r.outgoing.at[1, :, :, columns], r.core_in.at[:, :, columns], r.core_sems, n, partner
        )

    def return_column(n, d):
        columns = pl.ds(BLOCKS[n][0], BLOCKS[n][1] - BLOCKS[n][0])
        return remote(
            r.merged.at[d, :, columns],
            r.column_in.at[d - 1, :, columns],
            r.column_sems,
            n * 3 + d - 1,
            column_device(-d),
        )

    def merge(n):
        columns = slice(*BLOCKS[n])
        return_core(n).wait_recv()
        for d in (2, 1, 3, 0):
            both = r.outgoing[0, d, :, columns].astype(jnp.float32) + r.core_in[d, :, columns].astype(
                jnp.float32
            )
            r.merged[d, :, columns] = both.astype(jnp.bfloat16)
        for d in (2, 1, 3):
            return_column(n, d).start()

    for n in range(len(BLOCKS)):
        columns = slice(*BLOCKS[n])
        width = BLOCKS[n][1] - BLOCKS[n][0]
        have("dn", BLOCKS[n])
        for e in range(2):
            produced = dot(r.hidden[e], r.dn[e, :, :, columns].reshape(FF, width))
            for d in range(4):
                rows = produced[d * PART : (d + 1) * PART] * r.slot_gates[e, (mp - d + 4) % 4]
                for side in range(2):
                    r.produced[d, side, e * SLOTS : (e + 1) * SLOTS, :width] = rows[
                        side * SLOTS : (side + 1) * SLOTS
                    ].astype(jnp.bfloat16)
            pump_for(0.8)
        for side in (1, 0):
            for d in range(4):
                back = dot(r.slots_back[(mp - d + 4) % 4, side], r.produced[d, side, :, :width])
                r.outgoing[side, d, :, columns] = back.astype(jnp.bfloat16)
            if side:
                return_core(n).start()
            pump_for(0.8)
        if n:
            merge(n - 1)
    merge(len(BLOCKS) - 1)
    for n in range(len(BLOCKS)):
        columns = slice(*BLOCKS[n])
        for d in (1, 2, 3):
            return_column(n, d).wait_recv()
        result = r.middle[:, columns].astype(jnp.float32) + r.merged[0, :, columns].astype(jnp.float32)
        for d in range(3):
            result = result + r.column_in[d, :, columns].astype(jnp.float32)
        r.out[:, columns] = result.astype(jnp.bfloat16)

    for copy in sent:
        copy.copy.wait_send()


LOADED = ("trainer_gateup", "trainer_down", "tokens", "pair_weight", "query_weight", "output_weight")
INPUTS = LOADED + ("segments", "gains", "routes", "gates")


def layer(*operands):
    moves = gather_moves(PIECES)
    program = gather_program(moves)
    bf, wide = jnp.bfloat16, jnp.float32
    buffers = dict(
        normed=pltpu.VMEM((ROWS, MODEL_WIDTH), bf),
        pairs=pltpu.VMEM((2, WINDOW + ROWS, 128), bf),
        queries=pltpu.VMEM((ROWS, 384), bf),
        attended=pltpu.VMEM((ROWS, 384), bf),
        projected=pltpu.VMEM((4, PART, MODEL_WIDTH), bf),
        projected_in=pltpu.VMEM((3, PART, MODEL_WIDTH), bf),
        routes_other=pltpu.VMEM((TOPK, ROWS), jnp.int32),
        gates_other=pltpu.VMEM((TOPK, ROWS), wide),
        slots=pltpu.VMEM((4, 2, 2 * SLOTS, PART), bf),
        slots_back=pltpu.VMEM((4, 2, PART, 2 * SLOTS), bf),
        slot_gates=pltpu.VMEM((2, 4, PART, 1), wide),
        middle=pltpu.VMEM((PART, MODEL_WIDTH), bf),
        states=pltpu.VMEM((2, 4, PART, MODEL_WIDTH), bf),
        routed=pltpu.VMEM((2, 4, PART, MODEL_WIDTH), bf),
        hidden=pltpu.VMEM((2, 4 * PART, FF), bf),
        produced=pltpu.VMEM((4, 2, 2 * SLOTS, max(b - a for a, b in BLOCKS)), bf),
        outgoing=pltpu.VMEM((2, 4, PART, MODEL_WIDTH), bf),
        core_in=pltpu.VMEM((4, PART, MODEL_WIDTH), bf),
        merged=pltpu.VMEM((4, PART, MODEL_WIDTH), bf),
        column_in=pltpu.VMEM((3, PART, MODEL_WIDTH), bf),
        gu=pltpu.VMEM((2, 16, 96, MODEL_WIDTH), bf),
        dn=pltpu.VMEM((2, 16, 48, MODEL_WIDTH), bf),
        load_sems=pltpu.SemaphoreType.DMA((len(LOADED),)),
    )
    for name, operand in zip(LOADED, operands):
        shape = operand.shape[1:] if name == "pair_weight" else operand.shape
        buffers[name + "_here"] = pltpu.VMEM(shape, operand.dtype)
    counts = dict(
        weight=len(moves), routing=2, pair=5, projected=3, state=3, across=4, core=len(BLOCKS), column=3 * len(BLOCKS)
    )
    for name, count in counts.items():
        buffers[name + "_send"] = pltpu.SemaphoreType.DMA((count,))
        buffers[name + "_recv"] = pltpu.SemaphoreType.DMA((count,))
    names = INPUTS + ("out",) + tuple(buffers)

    def kernel(*refs):
        found = dict(zip(names, refs))
        for name in counts:
            found[name + "_sems"] = (found[name + "_send"], found[name + "_recv"])
        layer_kernel(moves, program, types.SimpleNamespace(**found))

    return pl.pallas_call(
        kernel,
        out_shape=jax.ShapeDtypeStruct((PART, MODEL_WIDTH), bf),
        in_specs=[
            pl.BlockSpec(memory_space=pl.ANY if name in LOADED else pltpu.VMEM) for name in INPUTS
        ],
        out_specs=pl.BlockSpec(memory_space=pltpu.VMEM),
        scratch_shapes=list(buffers.values()),
        compiler_params=pltpu.CompilerParams(
            collective_id=0, has_side_effects=True, vmem_limit_bytes=66_000_000
        ),
    )(*operands)


def body(
    tokens,
    segments,
    norm_gains,
    query_weight,
    key_value_matrix,
    output_weight,
    trainer_gateup,
    trainer_down,
    routes,
    route_weights,
):
    out = layer(
        trainer_gateup[0],
        trainer_down[0],
        tokens,
        key_value_matrix,
        query_weight,
        output_weight,
        segments.reshape(-1, 128),
        norm_gains,
        routes.T,
        route_weights.T,
    )
    return out.reshape(1, 1, PART, MODEL_WIDTH)


def solution(mesh):
    in_specs = (
        P(("dp", "expert"), None),
        P(),
        P(),
        P(None, "mp"),
        P(),
        P("mp", None),
        P(("mp", "expert"), "dp", None),
        P(("mp", "expert"), "dp", None),
        P(("dp", "expert"), None),
        P(("dp", "expert"), None),
    )
    out_specs = P(("dp", "expert"), "mp", None, None)
    return jax.shard_map(body, mesh=mesh, in_specs=in_specs, out_specs=out_specs, check_vma=False)
```

```python
import functools
import heapq
import math
import types

import jax
import jax.numpy as jnp
from jax import lax
from jax.experimental import pallas as pl
from jax.experimental.pallas import tpu as pltpu
from jax.sharding import PartitionSpec as P

MODEL_WIDTH = 1536
FF = 768
TOPK = 4


LINKS = ("y+", "y-", "z+", "z-")
AXES = ("dp", "mp", "expert")
MESH = pl.DeviceIdType.MESH


def column_ring(moves, rank, tag, piece, halves, dy, have):
    got = {0: have}
    up, down = have, have
    for s in range(1, 4):
        moves.append(("z+", (dy, 1 - s), piece, up, (rank, tag, s)))
        up = got[-s] = [len(moves) - 1]
        moves.append(("z-", (dy, s - 1), piece, down, (rank, tag, s)))
        down = got[s] = [len(moves) - 1]
    moves.append(("z+", (dy, -3), halves[0], up, (rank, tag, 4)))
    moves.append(("z-", (dy, 3), halves[1], down, (rank, tag, 4)))
    got[4] = [len(moves) - 2, len(moves) - 1]
    return got


def row_ring(moves, rank, tag, piece, halves, dz, have, late):
    start = len(moves)
    moves.append(("y+", (0, dz), piece, have, (rank, tag, 1 + late)))
    moves.append(("y-", (0, dz), piece, have, (rank, tag, 1 + late)))
    moves.append(("y+", (-1, dz), halves[0], [start], (rank, tag, 2 + late)))
    moves.append(("y-", (1, dz), halves[1], [start + 1], (rank, tag, 2 + late)))
    return {0: have, -1: [start], 1: [start + 1], 2: [start + 2, start + 3]}


def gather_moves(pieces):
    moves = []
    for rank, order, piece, halves in pieces:
        if order == "zy":
            got = column_ring(moves, rank, 0, piece, halves, 0, [])
            for late, dz in enumerate((0, -1, 1, -2, 2, -3, 3, 4)):
                row_ring(moves, rank, 1, piece, halves, dz, got[dz], late)
        else:
            got = row_ring(moves, rank, 0, piece, halves, 0, [], 0)
            for late, dy in enumerate((0, -1, 1, 2)):
                column_ring(moves, rank, 1 + late, piece, halves, dy, got[dy])
    return moves


def gather_program(moves, rate=40e3, latency=1.7):
    issued, got = set(), set()
    free = dict.fromkeys(LINKS, 0.0)
    arrivals, now, program = [], 0.0, []
    while True:
        for link in LINKS:
            while True:
                ready = [
                    (moves[i][4], i)
                    for i in range(len(moves))
                    if moves[i][0] == link and i not in issued and got.issuperset(moves[i][3])
                ]
                if not ready:
                    break
                (rank, _, _), i = min(ready)
                if free[link] - now > (AHEAD_FIRST if rank == 0 else AHEAD):
                    break
                _, r0, r1, c0, c1 = moves[i][2]
                issued.add(i)
                program.append(("send", i, now))
                free[link] = max(now, free[link]) + (r1 - r0) * (c1 - c0) * 2 / rate
                heapq.heappush(arrivals, (free[link] + latency, i))
        if not arrivals:
            return program
        now, i = heapq.heappop(arrivals)
        got.add(i)
        program.append(("recv", i, now))


PIECES = (
    (0, "zy", ("gu", 0, 64, 0, 1536), (("gu", 0, 32, 0, 1536), ("gu", 32, 64, 0, 1536))),
    (0, "yz", ("gu", 64, 96, 0, 1536), (("gu", 64, 80, 0, 1536), ("gu", 80, 96, 0, 1536))),
    (1, "zy", ("dn", 0, 48, 0, 768), (("dn", 0, 48, 0, 384), ("dn", 0, 48, 384, 768))),
    (1, "yz", ("dn", 0, 48, 768, 1536), (("dn", 0, 48, 768, 1152), ("dn", 0, 48, 1152, 1536))),
)
AHEAD_FIRST = 30.0
AHEAD = 12.0
PUMP = {
    "start": 0.1, "pairs": 4.4, "query": 6.6, "onward": 13.3, "window": 19.9,
    "a00": 21.0, "a01": 22.1, "a02": 23.2, "a10": 24.3, "a11": 25.4, "a12": 26.5, "a20": 27.6, "a21": 28.7, "a22": 29.8,
    "project": 32.0, "slots": 35.4, "partial": 44.2, "middle": 47.5,
    "g0": 49.7, "g1": 60.5, "g2": 65.5, "g3": 69.2,
}

ROWS = 384
PART = 96
SLOTS = 48
WINDOW = 1152
F_CHUNK = 256
BLOCKS = ((0, 512), (512, 896), (896, 1152), (1152, 1408), (1408, 1536))


def dot(a, b):
    return jnp.dot(a, b, preferred_element_type=jnp.float32)


def layer_kernel(moves, program, refs):
    r = refs
    dp, mp, expert = (lax.axis_index(a) for a in AXES)
    y, z_lo, z_hi, core = dp // 4, dp % 4, expert // 2, expert % 2
    z = z_hi * 4 + z_lo
    group = dp * 4 + expert

    def place(dy, dz):
        other_y, other_z = (y + dy + 8) % 4, (z + dz + 8) % 8
        return other_z // 4, other_y * 4 + other_z % 4

    def grid_device(dy, dz):
        half, index = place(dy, dz)
        return (index, mp, half * 2 + core)

    def column_device(d):
        return (dp, (mp + d + 4) % 4, expert)

    def piece_device(d):
        other = (group + d + 64) % 64
        return (other // 4, mp, other % 4)

    partner = (dp, mp, z_hi * 2 + 1 - core)
    target = {"y+": (1, 0), "y-": (-1, 0), "z+": (0, 1), "z-": (0, -1)}

    barrier = pltpu.get_barrier_semaphore()
    greeted = [grid_device(*target[link]) for link in LINKS]
    beside = (dp, mp + 1 - 2 * (mp % 2), expert)
    across = (dp, mp + 1 - 2 * (mp % 2), z_hi * 2 + 1 - core)
    greeted += [column_device(d) for d in (1, 2, 3)] + [partner, across]
    greeted += [piece_device(-2), piece_device(2 * core - 3)]
    for other in greeted:
        pl.semaphore_signal(barrier, inc=1, device_id=other, device_id_type=MESH)
    sent = []

    class Transfer:
        def __init__(self, start, landing, sems, i, device):
            self.copy = pltpu.make_async_remote_copy(
                src_ref=start,
                dst_ref=landing,
                send_sem=sems[0].at[i],
                recv_sem=sems[1].at[i],
                device_id=device,
                device_id_type=MESH,
            )

        def start(self):
            self.copy.start()
            sent.append(self)

        def wait_recv(self):
            self.copy.wait_recv()

    remote = Transfer

    whole = {"gu": r.gu, "dn": r.dn}

    def weight_copy(i):
        link, (dy, dz), (name, r0, r1, c0, c1), _, _ = moves[i]
        half, index = place(dy, dz)
        slab = whole[name].at[half, index, pl.ds(r0, r1 - r0), pl.ds(c0, c1 - c0)]
        return remote(slab, slab, r.weight_sems, i, grid_device(*target[link]))

    position = [0]

    def advance(stop):
        while position[0] < len(program) and not stop(program[position[0]]):
            kind, i, _ = program[position[0]]
            if kind == "send":
                weight_copy(i).start()
            else:
                weight_copy(i).wait_recv()
            position[0] += 1

    def pump(name):
        advance(lambda step: step[2] > PUMP[name])

    def pump_for(span):
        if position[0] < len(program):
            end = program[position[0]][2] + span
            advance(lambda step: step[2] > end)

    def have(name, columns):
        needed = {
            i for i, move in enumerate(moves)
            if move[2][0] == name and move[2][3] < columns[1] and columns[0] < move[2][4]
        }
        needed -= {i for kind, i, _ in program[: position[0]] if kind == "recv"}

        def stop(step):
            if not needed:
                return True
            if step[0] == "recv":
                needed.discard(step[1])
            return False

        advance(stop)

    half, index = place(0, 0)
    arriving = {}
    for k, name in enumerate(LOADED):
        start = getattr(r, name)
        if name == "pair_weight":
            start = start.at[mp // 2]
        arriving[name] = pltpu.make_async_copy(start, getattr(r, name + "_here"), r.load_sems.at[k])
        arriving[name].start()
    arriving["trainer_gateup"].wait()
    r.gu[half, index] = r.trainer_gateup_here[...].astype(jnp.bfloat16)
    arriving["trainer_down"].wait()
    r.dn[half, index] = r.trainer_down_here[...].astype(jnp.bfloat16)
    barrier = pltpu.get_barrier_semaphore()
    pl.semaphore_wait(barrier, len(greeted))
    routing = [
        remote(here, there, r.routing_sems, k, partner)
        for k, (here, there) in enumerate(((r.routes, r.routes_other), (r.gates, r.gates_other)))
    ]
    for copy in routing:
        copy.start()
    pump("start")

    arriving["tokens"].wait()
    gain = r.gains[0:1, :]

    @pl.loop(0, ROWS // 32)
    def _(i):
        rows = pl.ds(pl.multiple_of(i * 32, 32), 32)
        wide = r.tokens_here[rows, :].astype(jnp.float32)
        scale = lax.rsqrt(jnp.mean(wide * wide, axis=-1, keepdims=True) + 1e-6)
        r.normed[rows, :] = (wide * scale * gain).astype(jnp.bfloat16)

    arriving["pair_weight"].wait()
    pair = dot(r.normed[...], r.pair_weight_here[...]).astype(jnp.bfloat16)
    for part in range(2):
        r.pairs[part, WINDOW:, :] = pair[:, part * 128 : (part + 1) * 128]

    half_here = mp % 2

    def piece_rows(k):
        return pl.ds(pl.multiple_of(k * ROWS, ROWS), ROWS)

    onward = remote(
        r.pairs.at[half_here, piece_rows(3)], r.pairs.at[half_here, piece_rows(1)], r.pair_sems, 0, piece_device(2)
    )
    direct = remote(
        r.pairs.at[:, piece_rows(3)],
        r.pairs.at[:, piece_rows(2 - 2 * core)],
        r.pair_sems,
        1,
        piece_device(1 + 2 * core),
    )
    landed = r.pairs.at[half_here, piece_rows(1)]
    crossing = r.pairs.at[half_here, piece_rows(2 * core)]
    shares = [
        remote(landed, landed, r.pair_sems, 2, beside),
        remote(landed, crossing, r.pair_sems, 3, partner),
        remote(landed, crossing, r.pair_sems, 4, across),
    ]
    onward.start()
    direct.start()
    pump("pairs")
    arriving["query_weight"].wait()
    r.queries[...] = dot(r.normed[...], r.query_weight_here[...]).astype(jnp.bfloat16)
    pump("query")

    lanes = []
    for k in range(12):
        row = (group * 3 - 9 + k + 192) % 192
        lanes.append(r.segments[pl.ds(row, 1), :])
    key_segment = jnp.concatenate(lanes, axis=1)
    diagonal = lax.broadcasted_iota(jnp.int32, (128, 128), 0) == lax.broadcasted_iota(
        jnp.int32, (128, 128), 1
    )
    first_key = (group - 3) * ROWS

    pump("onward")
    onward.wait_recv()
    for copy in shares:
        copy.start()
    pump("window")
    for copy in shares + [direct]:
        copy.wait_recv()
    for c in range(3):
        low = (c + 1) * 128
        own_lanes = jnp.broadcast_to(lanes[9 + c].astype(jnp.float32), (128, 128))
        query_segment = jnp.sum(jnp.where(diagonal, own_lanes, 0.0), axis=1, keepdims=True)
        key_offset = low + lax.broadcasted_iota(jnp.int32, (128, WINDOW), 1)
        query_offset = WINDOW + c * 128 + lax.broadcasted_iota(jnp.int32, (128, WINDOW), 0)
        allowed = (
            (key_segment[:, low : low + WINDOW].astype(jnp.float32) == query_segment)
            & (key_offset <= query_offset)
            & (key_offset + first_key >= 0)
        )
        keys = r.pairs[0, low : low + WINDOW, :]
        values = r.pairs[1, low : low + WINDOW, :]
        for h in range(3):
            query = r.queries[c * 128 : (c + 1) * 128, h * 128 : (h + 1) * 128]
            scores = lax.dot_general(
                query, keys, (((1,), (1,)), ((), ())), preferred_element_type=jnp.float32
            )
            scores = jnp.where(allowed, scores * (1.0 / math.sqrt(128)), -1e30)
            weights = jnp.exp(scores - jnp.max(scores, axis=1, keepdims=True))
            total = jnp.sum(weights, axis=1, keepdims=True)
            mixed = dot(weights.astype(jnp.bfloat16), values) / total
            r.attended[c * 128 : (c + 1) * 128, h * 128 : (h + 1) * 128] = mixed.astype(jnp.bfloat16)
            pump(f"a{c}{h}")

    def partial_copy(d):
        return remote(
            r.projected.at[(mp + d) % 4], r.projected_in.at[d - 1], r.projected_sems, d - 1, column_device(d)
        )

    arriving["output_weight"].wait()
    r.projected[...] = (
        dot(r.attended[...], r.output_weight_here[...]).astype(jnp.bfloat16).reshape(4, PART, MODEL_WIDTH)
    )
    for d in (2, 1, 3):
        partial_copy(d).start()
    pump("project")

    for copy in routing:
        copy.wait_recv()
    before = lax.broadcasted_iota(jnp.int32, (ROWS, ROWS), 0)
    token = lax.broadcasted_iota(jnp.int32, (ROWS, ROWS), 1)
    earlier = ((before < token) & (before // PART == token // PART)).astype(jnp.bfloat16)
    slot = lax.broadcasted_iota(jnp.int32, (SLOTS, ROWS), 0).astype(jnp.float32)
    for side, (routes, gates) in enumerate(((r.routes, r.gates), (r.routes_other, r.gates_other))):
        picks = []
        for e in range(2):
            named = routes[...] == mp * 4 + e * 2 + core
            hit = jnp.sum(jnp.where(named, 1.0, 0.0), axis=0, keepdims=True)
            gate = jnp.sum(jnp.where(named, gates[...], 0.0), axis=0, keepdims=True)
            rank = dot(jnp.broadcast_to(hit, (8, ROWS)).astype(jnp.bfloat16), earlier)[0:1, :]
            chosen = jnp.where((slot == rank) & (hit > 0.5), 1.0, 0.0)
            picks.append(chosen)
            weighed = chosen * gate
            for m in range(4):
                lanes = slice(m * PART, (m + 1) * PART)
                r.slots[m, side, e * SLOTS : (e + 1) * SLOTS, :] = chosen[:, lanes].astype(jnp.bfloat16)
                r.slot_gates[e, m, side * SLOTS : (side + 1) * SLOTS, :] = jnp.sum(
                    weighed[:, lanes], axis=1, keepdims=True
                )
        for m in range(4):
            both = jnp.concatenate([chosen[:, m * PART : (m + 1) * PART] for chosen in picks], axis=0)
            r.slots_back[m, side] = both.T.astype(jnp.bfloat16)
    pump("slots")
    pump("partial")

    for d in (1, 2, 3):
        partial_copy(d).wait_recv()
    summed = r.tokens_here[pl.ds(pl.multiple_of(mp * PART, PART), PART), :].astype(jnp.float32)
    attention = r.projected[mp].astype(jnp.float32)
    for d in range(3):
        attention = attention + r.projected_in[d].astype(jnp.float32)
    middle = (summed + attention).astype(jnp.bfloat16)
    r.middle[...] = middle
    wide = middle.astype(jnp.float32)
    scale = lax.rsqrt(jnp.mean(wide * wide, axis=-1, keepdims=True) + 1e-6)
    r.states[0, 0] = (wide * scale * r.gains[1:2, :]).astype(jnp.bfloat16)

    def state_copy(d):
        return remote(r.states.at[0, 0], r.states.at[0, d], r.state_sems, d - 1, column_device(d))

    def across_copy(d):
        return remote(r.states.at[0, d], r.states.at[1, d], r.across_sems, d, partner)

    for d in (2, 1, 3):
        state_copy(d).start()
    across_copy(0).start()
    pump("middle")
    for step, d in enumerate((0, 1, 3, 2)):
        pump(f"g{step}")
        if d:
            state_copy(d).wait_recv()
            across_copy(d).start()
        for side in range(2):
            if side:
                across_copy(d).wait_recv()
            picked = dot(r.slots[(mp - d + 4) % 4, side], r.states[side, d]).astype(jnp.bfloat16)
            for e in range(2):
                r.routed[e, d, side * SLOTS : (side + 1) * SLOTS, :] = picked[e * SLOTS : (e + 1) * SLOTS]

    have("gu", (0, MODEL_WIDTH))
    for e in range(2):
        inputs = r.routed[e].reshape(4 * PART, MODEL_WIDTH)
        for f in range(3):
            left = f * F_CHUNK
            gate = dot(inputs, r.gu[e, :, :, left : left + F_CHUNK].reshape(MODEL_WIDTH, F_CHUNK))
            rise = dot(inputs, r.gu[e, :, :, FF + left : FF + left + F_CHUNK].reshape(MODEL_WIDTH, F_CHUNK))
            r.hidden[e, :, left : left + F_CHUNK] = (jnp.maximum(gate, 0.0) * rise).astype(jnp.bfloat16)
            pump_for(0.7)

    def return_core(n):
        columns = pl.ds(BLOCKS[n][0], BLOCKS[n][1] - BLOCKS[n][0])
        return remote(
            r.outgoing.at[1, :, :, columns], r.core_in.at[:, :, columns], r.core_sems, n, partner
        )

    def return_column(n, d):
        columns = pl.ds(BLOCKS[n][0], BLOCKS[n][1] - BLOCKS[n][0])
        return remote(
            r.merged.at[d, :, columns],
            r.column_in.at[d - 1, :, columns],
            r.column_sems,
            n * 3 + d - 1,
            column_device(-d),
        )

    def merge(n):
        columns = slice(*BLOCKS[n])
        return_core(n).wait_recv()
        for d in (2, 1, 3, 0):
            both = r.outgoing[0, d, :, columns].astype(jnp.float32) + r.core_in[d, :, columns].astype(
                jnp.float32
            )
            r.merged[d, :, columns] = both.astype(jnp.bfloat16)
        for d in (2, 1, 3):
            return_column(n, d).start()

    for n in range(len(BLOCKS)):
        columns = slice(*BLOCKS[n])
        width = BLOCKS[n][1] - BLOCKS[n][0]
        have("dn", BLOCKS[n])
        for e in range(2):
            produced = dot(r.hidden[e], r.dn[e, :, :, columns].reshape(FF, width))
            for d in range(4):
                rows = produced[d * PART : (d + 1) * PART] * r.slot_gates[e, (mp - d + 4) % 4]
                for side in range(2):
                    r.produced[d, side, e * SLOTS : (e + 1) * SLOTS, :width] = rows[
                        side * SLOTS : (side + 1) * SLOTS
                    ].astype(jnp.bfloat16)
            pump_for(0.8)
        for side in (1, 0):
            for d in range(4):
                back = dot(r.slots_back[(mp - d + 4) % 4, side], r.produced[d, side, :, :width])
                r.outgoing[side, d, :, columns] = back.astype(jnp.bfloat16)
            if side:
                return_core(n).start()
            pump_for(0.8)
        if n:
            merge(n - 1)
    merge(len(BLOCKS) - 1)
    for n in range(len(BLOCKS)):
        columns = slice(*BLOCKS[n])
        for d in (1, 2, 3):
            return_column(n, d).wait_recv()
        result = r.middle[:, columns].astype(jnp.float32) + r.merged[0, :, columns].astype(jnp.float32)
        for d in range(3):
            result = result + r.column_in[d, :, columns].astype(jnp.float32)
        r.out[:, columns] = result.astype(jnp.bfloat16)

    for copy in sent:
        copy.copy.wait_send()


LOADED = ("trainer_gateup", "trainer_down", "tokens", "pair_weight", "query_weight", "output_weight")
INPUTS = LOADED + ("segments", "gains", "routes", "gates")


def layer(*operands):
    moves = gather_moves(PIECES)
    program = gather_program(moves)
    bf, wide = jnp.bfloat16, jnp.float32
    buffers = dict(
        normed=pltpu.VMEM((ROWS, MODEL_WIDTH), bf),
        pairs=pltpu.VMEM((2, WINDOW + ROWS, 128), bf),
        queries=pltpu.VMEM((ROWS, 384), bf),
        attended=pltpu.VMEM((ROWS, 384), bf),
        projected=pltpu.VMEM((4, PART, MODEL_WIDTH), bf),
        projected_in=pltpu.VMEM((3, PART, MODEL_WIDTH), bf),
        routes_other=pltpu.VMEM((TOPK, ROWS), jnp.int32),
        gates_other=pltpu.VMEM((TOPK, ROWS), wide),
        slots=pltpu.VMEM((4, 2, 2 * SLOTS, PART), bf),
        slots_back=pltpu.VMEM((4, 2, PART, 2 * SLOTS), bf),
        slot_gates=pltpu.VMEM((2, 4, PART, 1), wide),
        middle=pltpu.VMEM((PART, MODEL_WIDTH), bf),
        states=pltpu.VMEM((2, 4, PART, MODEL_WIDTH), bf),
        routed=pltpu.VMEM((2, 4, PART, MODEL_WIDTH), bf),
        hidden=pltpu.VMEM((2, 4 * PART, FF), bf),
        produced=pltpu.VMEM((4, 2, 2 * SLOTS, max(b - a for a, b in BLOCKS)), bf),
        outgoing=pltpu.VMEM((2, 4, PART, MODEL_WIDTH), bf),
        core_in=pltpu.VMEM((4, PART, MODEL_WIDTH), bf),
        merged=pltpu.VMEM((4, PART, MODEL_WIDTH), bf),
        column_in=pltpu.VMEM((3, PART, MODEL_WIDTH), bf),
        gu=pltpu.VMEM((2, 16, 96, MODEL_WIDTH), bf),
        dn=pltpu.VMEM((2, 16, 48, MODEL_WIDTH), bf),
        load_sems=pltpu.SemaphoreType.DMA((len(LOADED),)),
    )
    for name, operand in zip(LOADED, operands):
        shape = operand.shape[1:] if name == "pair_weight" else operand.shape
        buffers[name + "_here"] = pltpu.VMEM(shape, operand.dtype)
    counts = dict(
        weight=len(moves), routing=2, pair=5, projected=3, state=3, across=4, core=len(BLOCKS), column=3 * len(BLOCKS)
    )
    for name, count in counts.items():
        buffers[name + "_send"] = pltpu.SemaphoreType.DMA((count,))
        buffers[name + "_recv"] = pltpu.SemaphoreType.DMA((count,))
    names = INPUTS + ("out",) + tuple(buffers)

    def kernel(*refs):
        found = dict(zip(names, refs))
        for name in counts:
            found[name + "_sems"] = (found[name + "_send"], found[name + "_recv"])
        layer_kernel(moves, program, types.SimpleNamespace(**found))

    return pl.pallas_call(
        kernel,
        out_shape=jax.ShapeDtypeStruct((PART, MODEL_WIDTH), bf),
        in_specs=[
            pl.BlockSpec(memory_space=pl.ANY if name in LOADED else pltpu.VMEM) for name in INPUTS
        ],
        out_specs=pl.BlockSpec(memory_space=pltpu.VMEM),
        scratch_shapes=list(buffers.values()),
        compiler_params=pltpu.CompilerParams(
            collective_id=0, has_side_effects=True, vmem_limit_bytes=66_000_000
        ),
    )(*operands)


def body(
    tokens,
    segments,
    norm_gains,
    query_weight,
    key_value_matrix,
    output_weight,
    trainer_gateup,
    trainer_down,
    routes,
    route_weights,
):
    out = layer(
        trainer_gateup[0],
        trainer_down[0],
        tokens,
        key_value_matrix,
        query_weight,
        output_weight,
        segments.reshape(-1, 128),
        norm_gains,
        routes.T,
        route_weights.T,
    )
    return out.reshape(1, 1, PART, MODEL_WIDTH)


def solution(mesh):
    in_specs = (
        P(("dp", "expert"), None),
        P(),
        P(),
        P(None, "mp"),
        P(),
        P("mp", None),
        P(("mp", "expert"), "dp", None),
        P(("mp", "expert"), "dp", None),
        P(("dp", "expert"), None),
        P(("dp", "expert"), None),
    )
    out_specs = P(("dp", "expert"), "mp", None, None)
    return jax.shard_map(body, mesh=mesh, in_specs=in_specs, out_specs=out_specs, check_vma=False)
```
